512 devices in a mesh: expert: 128 (over y, x, z_lo), hidden: 4 (over z_hi, core).
Axes of the slice: x: 4, y: 4, z: 16 (z_hi: 2, z_lo: 8; z = z_hi * 8 + z_lo), core: 2. Of those that a mesh axis runs over, the one named last changes fastest.
Arguments:
- tokens: bfloat16 [256, 196, 1024], P('expert', None, 'hidden'), may hold values from -64 to 64
- slot_params: bfloat16 [1024, 128], P('hidden'), may hold values from -0.4 to 0.4
- weight_in: bfloat16 [128, 1024, 4096], P('expert', None, 'hidden'), may hold values from -0.1875 to 0.1875
- bias_in: bfloat16 [128, 4096], P('expert', 'hidden'), may hold values from -3 to 3
- weight_out: bfloat16 [128, 4096, 1024], P('expert', 'hidden'), may hold values from -0.09375 to 0.09375
- bias_out: bfloat16 [128, 1024], P('expert', 'hidden'), may hold values from -3 to 3
- cotangent: bfloat16 [256, 196, 1024], P('expert', None, 'hidden'), may hold values from -1.5 to 1.5
Outputs:
- mixed: bfloat16 [256, 196, 1024], P('expert', None, 'hidden')
- token_grad: bfloat16 [256, 196, 1024], P('expert', None, 'hidden')
- zloss: float32 [256, 196], P('expert')
The draws below stay inside these ranges and needn't reach their ends.
All inputs are finite; a program needn't handle non-finite values.
Results may differ from the reference program's by a relative error of at most 0.015.
Values may be sent and summed in bfloat16 or wider, within the bound.
A program may use at most 64 MiB of HBM per device.

```python
import jax
import jax.numpy as jnp
from jax import lax

D = 1024
FF = 4096
TOK = 196
EXPERTS = 128
IMAGES = 256


def shared_params(key):
    base = jax.random.fold_in(key, 11)
    return 0.0625 * jnp.clip(jax.random.normal(base, (D, EXPERTS), jnp.float32), -6.0, 6.0)


def draw_slot_params(key, part):
    return shared_params(key).astype(jnp.bfloat16)


def draw_tokens(key, part):
    values = jnp.clip(jax.random.normal(jax.random.fold_in(key, 12), (IMAGES, TOK, D), jnp.float32), -6.0, 6.0)
    return values.astype(jnp.bfloat16)


def block_levels(own_key, dims, pieces, smallest, top_value):
    factor_of, own = 1.0, jax.random.fold_in(own_key, 6)
    for dim, parts in pieces:
        steps = jnp.exp(jax.random.uniform(jax.random.fold_in(own, dim), (parts,), jnp.float32, smallest / len(pieces), top_value / len(pieces)))
        factor_of = factor_of * jnp.repeat(steps, dims[dim] // parts).reshape([-1 if axis == dim else 1 for axis in range(len(dims))])
    return factor_of


def centred(rng, dims, width, reach, split=(), dtype=jnp.bfloat16):
    values = width * jax.random.normal(rng, dims, jnp.float32)
    if split:
        values = values * block_levels(rng, dims, split, -0.22, 0.18)
    return jnp.clip(values, -reach, reach).astype(dtype)


def setup_inputs(seed: int = 0) -> dict:
    seeds = jax.random.split(jax.random.key(seed), 8)
    return {
        "tokens": draw_tokens(jax.random.fold_in(seeds[7], 71), 0),
        "slot_params": draw_slot_params(jax.random.fold_in(seeds[7], 71), 0),
        "weight_in": centred(seeds[2], (EXPERTS, D, FF), D ** -0.5, 0.1875, ((0, 128), (2, 4))),
        "bias_in": centred(seeds[3], (EXPERTS, FF), 0.5, 3.0, ((0, 128), (1, 4))),
        "weight_out": centred(seeds[4], (EXPERTS, FF, D), FF ** -0.5, 0.09375, ((0, 128), (1, 4))),
        "bias_out": centred(seeds[5], (EXPERTS, D), 0.5, 3.0, ((0, 128), (1, 4))),
        "cotangent": centred(seeds[6], (IMAGES, TOK, D), 0.25, 1.5, ((0, 128), (2, 4))),
    }


loss_weight = 0.1


def gelu_parts(value):
    factor = 0.7978845608028654
    inner = factor * (value + 0.044715 * value * value * value)
    slope_tanh = jnp.tanh(inner)
    result = 0.5 * value * (1.0 + slope_tanh)
    slope = 0.5 * (1.0 + slope_tanh) + 0.5 * value * (1.0 - slope_tanh * slope_tanh) * factor * (1.0 + 3.0 * 0.044715 * value * value)
    return result, slope


def expert_step(inputs):
    slot_in, out_grad, w_first, b_first, w_second, b_second = inputs
    pre_act = jnp.dot(slot_in, w_first, preferred_element_type=jnp.float32) + b_first.astype(jnp.float32)
    activated, slope = gelu_parts(pre_act)
    act_low = activated.astype(jnp.bfloat16)
    slot_out = (jnp.dot(act_low, w_second, preferred_element_type=jnp.float32) + b_second.astype(jnp.float32)).astype(jnp.bfloat16)
    hidden_grad = jnp.dot(out_grad, w_second.T, preferred_element_type=jnp.float32)
    pre_grad = (hidden_grad * slope).astype(jnp.bfloat16)
    in_grad = jnp.dot(pre_grad, w_first.T, preferred_element_type=jnp.float32).astype(jnp.bfloat16)
    return slot_out, in_grad


def reference(tokens, slot_params, weight_in, bias_in, weight_out, bias_out, cotangent):
    tokens_wide = tokens.astype(jnp.float32)
    params_wide = slot_params.astype(jnp.float32)
    grad_wide = cotangent.astype(jnp.float32)
    logits = jnp.einsum("itd,ds->its", tokens_wide, params_wide)
    dispatch = jax.nn.softmax(logits, axis=1)
    combine = jax.nn.softmax(logits, axis=2)
    log_total = jax.nn.logsumexp(logits, axis=2)
    zloss = loss_weight * log_total * log_total
    dispatch_low = dispatch.astype(jnp.bfloat16)
    combine_low = combine.astype(jnp.bfloat16)
    slot_in = jnp.einsum("its,itd->isd", dispatch_low.astype(jnp.float32), tokens_wide).astype(jnp.bfloat16)
    out_grad = jnp.einsum("its,itd->isd", combine_low.astype(jnp.float32), grad_wide).astype(jnp.bfloat16)
    slot_out, in_grad = lax.map(expert_step, (jnp.transpose(slot_in, (1, 0, 2)), jnp.transpose(out_grad, (1, 0, 2)), weight_in, bias_in, weight_out, bias_out))
    slot_out = jnp.transpose(slot_out, (1, 0, 2)).astype(jnp.float32)
    in_grad = jnp.transpose(in_grad, (1, 0, 2)).astype(jnp.float32)
    mixed = jnp.einsum("its,isd->itd", combine_low.astype(jnp.float32), slot_out).astype(jnp.bfloat16)
    combine_grad = jnp.einsum("itd,isd->its", grad_wide, slot_out)
    dispatch_grad = jnp.einsum("itd,isd->its", tokens_wide, in_grad)
    from_combine = combine * (combine_grad - jnp.sum(combine * combine_grad, axis=2, keepdims=True)) + 2.0 * loss_weight * log_total[:, :, None] * combine
    from_dispatch = dispatch * (dispatch_grad - jnp.sum(dispatch * dispatch_grad, axis=1, keepdims=True))
    logit_grad = (from_combine + from_dispatch).astype(jnp.bfloat16).astype(jnp.float32)
    token_grad = jnp.einsum("its,ds->itd", logit_grad, params_wide) + jnp.einsum("its,isd->itd", dispatch_low.astype(jnp.float32), in_grad)
    return mixed, token_grad.astype(jnp.bfloat16), zloss
```

```python
import jax
import jax.numpy as jnp
from jax import lax
from jax.experimental import pallas as pl
from jax.experimental.pallas import tpu as pltpu
from jax.sharding import PartitionSpec as P

loss_weight = 0.1
MESH = pl.DeviceIdType.MESH
F32, BF16 = jnp.float32, jnp.bfloat16

IMG, TOK, TP, HALF, QF, SLOTS = 2, 196, 208, 104, 256, 128
NJ, NZ, NZL = 16, 16, 8


def gelu_parts(value):
    factor = 0.7978845608028654
    inner = factor * (value + 0.044715 * value * value * value)
    slope_tanh = jnp.tanh(inner)
    result = 0.5 * value * (1.0 + slope_tanh)
    slope = 0.5 * (1.0 + slope_tanh) + 0.5 * value * (1.0 - slope_tanh * slope_tanh) * factor * (
        1.0 + 3.0 * 0.044715 * value * value
    )
    return result, slope


def dot(a, b, ca, cb):
    return lax.dot_general(a, b, (((ca,), (cb,)), ((), ())), preferred_element_type=F32)


def kernel(
    tok, sp, w1_hbm, bi, w2_hbm, bo, cot,
    mixed, tgrad, zloss,
    w1, w2, wsem,
    lp, la, lzs, lzr, lf,
    disp, comb, tcomb, dlow, clow,
    s, r1, fa, r2, x,
    act, slope, px_s, px_r, cs, y, fb, q, v,
    gp, ga, gzs, gzr, gf,
    a1s, a1r, a2s, a2r, a3s, a3r, b1s, b1r, b2s, b2r, fws, fwr,
    pxs, pxr, c1s, c1r, c2s, c2r, d1s, d1r, d2s, d2r, d3s, d3r,
):
    e, h = lax.axis_index("expert"), lax.axis_index("hidden")
    j, zl, zh, c = e // NZL, e % NZL, h // 2, h % 2
    z = zh * NZL + zl
    core_peer = (e, zh * 2 + 1 - c)
    z8_peer = (e, (1 - zh) * 2 + c)

    def z_at(d):
        return (z + d) % NZ

    def z_dev(zz):
        return (j * NZL + zz % NZL, (zz // NZL) * 2 + c)

    def j_at(d):
        yy, xx = (j // 4 + d // 4) % 4, (j % 4 + d % 4) % 4
        return yy * 4 + xx

    def j_from(d):
        yy, xx = (j // 4 + 4 - d // 4) % 4, (j % 4 + 4 - d % 4) % 4
        return yy * 4 + xx

    def j_dev(jj):
        return (jj * NZL + zl, h)

    def rc(src, dst, ss, rs, dev):
        return pltpu.make_async_remote_copy(
            src_ref=src, dst_ref=dst, send_sem=ss, recv_sem=rs, device_id=dev, device_id_type=MESH
        )

    def each(n, body, start=1):
        lax.fori_loop(start, n, lambda k, carry: (body(k), carry)[1], 0)

    barrier = pltpu.get_barrier_semaphore()
    pl.semaphore_signal(barrier, inc=1, device_id=core_peer, device_id_type=MESH)
    each(NZ, lambda d: pl.semaphore_signal(barrier, inc=1, device_id=z_dev(z_at(d)), device_id_type=MESH))
    each(NJ, lambda d: pl.semaphore_signal(barrier, inc=1, device_id=j_dev(j_at(d)), device_id_type=MESH))
    w1_copy = pltpu.make_async_copy(w1_hbm, w1, wsem.at[0])
    w2_copy = pltpu.make_async_copy(w2_hbm, w2, wsem.at[1])
    w1_copy.start()
    w2_copy.start()

    mine, theirs = pl.ds(pl.multiple_of(c * HALF, 8), HALF), pl.ds(pl.multiple_of((1 - c) * HALF, 8), HALF)

    for i in range(IMG):
        lp[i] = dot(tok[i], sp[...], 1, 0)
    pl.semaphore_wait(barrier, 1 + (NZ - 1) + (NJ - 1))

    def a1(i):
        return rc(lp.at[i, theirs], la.at[i], a1s.at[i], a1r.at[i], core_peer)

    def a2(i):
        return rc(lzs.at[i], lzr.at[i], a2s.at[i], a2r.at[i], z8_peer)

    def a3(i, rows):
        return rc(lf.at[i, rows], lf.at[i, rows], a3s.at[i], a3r.at[i], core_peer)

    def b1(i, d, src, dst):
        return rc(s.at[i, :, src], r1.at[i, :, dst], b1s.at[i, d], b1r.at[i, d], j_dev(j_at(d)))

    def b2(i, d, src, half, low):
        return rc(r2.at[i, src], x.at[i, half * 2 + c, low], b2s.at[i, d], b2r.at[i, d], z_dev(z_at(d)))

    def fwd(i, d, quarter, low):
        return rc(x.at[i, quarter, low], x.at[i, quarter, low], fws.at[i, d], fwr.at[i, d], core_peer)

    def px(i, t):
        return rc(px_s.at[i, t], px_r.at[i, t], pxs.at[i, t], pxr.at[i, t], core_peer)

    def c1(i, t, d, sh, sl, dh, dl):
        return rc(cs.at[i, t, sh, sl], y.at[i, t, dh, dl], c1s.at[i, t, d], c1r.at[i, t, d], z_dev(z_at(d)))

    def c2(i, t, d, src, dst):
        return rc(q.at[i, t, src], v.at[i, t, dst], c2s.at[i, t, d], c2r.at[i, t, d], j_dev(j_at(d)))

    def d1(i):
        return rc(gp.at[i, theirs], ga.at[i], d1s.at[i], d1r.at[i], core_peer)

    def d2(i):
        return rc(gzs.at[i], gzr.at[i], d2s.at[i], d2r.at[i], z8_peer)

    def d3(i, rows):
        return rc(gf.at[i, rows], gf.at[i, rows], d3s.at[i], d3r.at[i], core_peer)

    def logits_across(i):
        a1(i).wait_recv()
        lzs[i] = lp[i, mine] + la[i]
        a2(i).start()

    def logits_whole(i):
        a2(i).wait_recv()
        lf[i, mine] = lzs[i] + lzr[i]
        a3(i, mine).start()

    def softmaxes(i):
        a3(i, theirs).wait_recv()
        logits = lf[i]
        row = lax.broadcasted_iota(jnp.int32, (TP, SLOTS), 0)
        masked = jnp.where(row < TOK, logits, -1e30)
        top = jnp.max(masked, axis=0, keepdims=True)
        up = jnp.exp(masked - top)
        dispatch = up / jnp.sum(up, axis=0, keepdims=True)
        disp[i] = dispatch
        dispatch_low = dispatch.astype(BF16)
        dlow[i] = dispatch_low
        s[i, 0] = dot(dispatch_low, tok[i], 0, 0).reshape(NJ, 8, QF).astype(BF16)
        top = jnp.max(logits, axis=1, keepdims=True)
        up = jnp.exp(logits - top)
        below = jnp.sum(up, axis=1, keepdims=True)
        combine = up / below
        comb[i] = combine
        combine_low = combine.astype(BF16)
        clow[i] = combine_low
        s[i, 1] = dot(combine_low, cot[i], 0, 0).reshape(NJ, 8, QF).astype(BF16)
        each(NJ, lambda d: b1(i, d, j_at(d), j).start())
        r1[i, :, j] = s[i, :, j]
        total = top + jnp.log(below)
        tcomb[i] = (2.0 * loss_weight) * total * combine
        wide = jnp.broadcast_to(loss_weight * total * total, (TP, SLOTS))
        zloss[i] = jnp.transpose(wide)[0:8, :]

    def to_experts(i):
        each(NJ, lambda d: b1(i, d, j_at(d), j_from(d)).wait_recv())
        for t in range(2):
            rows = r1[i, t].astype(F32).reshape(SLOTS, QF)
            for lanes in range(2):
                fa[t, lanes] = rows[:, lanes * 128 : (lanes + 1) * 128]
        for low in range(NZL):
            for t in range(2):
                rows = [fa[t, lanes, pl.ds(low, NJ, stride=8), :] for lanes in range(2)]
                r2[i, low, t] = jnp.concatenate(rows, axis=1).astype(BF16)
        each(NZ, lambda d: b2(i, d, z_at(d) % NZL, zh, zl).start())
        x[i, h, zl] = r2[i, zl]

    def near_first(k):
        return lax.select(k % 2 == 1, (k + 1) // 2, NZ - k // 2)

    def arrive(i):
        fwd(i, 0, h, zl).start()

        def one(k):
            d = near_first(k)
            src = z_at(NZ - d)
            b2(i, d, z_at(d) % NZL, src // NZL, src % NZL).wait_recv()
            fwd(i, d, (src // NZL) * 2 + c, src % NZL).start()

        each(NZ, one)

        def other(d):
            src = z_at(NZ - d)
            fwd(i, d, (src // NZL) * 2 + 1 - c, src % NZL).wait_recv()

        each(NZ, other, 0)

    def rows_of(i, t):
        return jnp.concatenate([x[i, k, :, t].reshape(SLOTS, QF) for k in range(4)], axis=1)

    def quarter(k, core):
        return pl.ds(pl.multiple_of((k * 2 + core) * QF, QF), QF)

    FB = 256

    def expert(i):
        arrived = rows_of(i, 0)
        for f in range(0, 1024, FB):
            part = dot(arrived, w1[:, f : f + FB], 1, 0) + bi[:, f : f + FB].astype(F32)
            activated, slope_part = gelu_parts(part)
            act[0, :, f : f + FB] = activated.astype(BF16)
            slope[:, f : f + FB] = slope_part
        send_results(i, 0, lambda cols: dot(act[0], w2[:, cols], 1, 0))
        arrived = rows_of(i, 1)
        for f in range(0, 1024, FB):
            part = dot(arrived, w2[f : f + FB, :], 1, 1) * slope[:, f : f + FB]
            act[1, :, f : f + FB] = part.astype(BF16)
        send_results(i, 1, lambda cols: dot(act[1], w1[cols, :], 1, 1))

    def send_results(i, t, product):
        for k in range(2):
            px_s[i, t, k] = product(quarter(k, 1 - c)).astype(BF16)
        px(i, t).start()
        own = [product(quarter(k, c)) for k in range(2)]
        px(i, t).wait_recv()
        for k in range(2):
            total = own[k] + px_r[i, t, k].astype(F32)
            if t == 0:
                total = total + jnp.where(zh == k, 1.0, 0.0) * bo[...].astype(F32)
            cs[i, t, k] = total.reshape(NZL, NJ, QF).astype(BF16)
        each(NZ, lambda d: c1(i, t, d, z_at(d) // NZL, z_at(d) % NZL, zh, zl).start())
        y[i, t, zh, zl] = cs[i, t, zh, zl]

    def to_images(i, t):
        def arrived(d):
            src = z_at(NZ - d)
            c1(i, t, d, z_at(d) // NZL, z_at(d) % NZL, src // NZL, src % NZL).wait_recv()

        each(NZ, arrived)
        for low in range(NZL):
            rows = y[i, t, 0, low].astype(F32) + y[i, t, 1, low].astype(F32)
            for lanes in range(2):
                fb[t, lanes, pl.ds(low, NJ, stride=8), :] = rows[:, lanes * 128 : (lanes + 1) * 128]
        rows = jnp.concatenate([fb[t, lanes] for lanes in range(2)], axis=1)
        q[i, t] = rows.reshape(NJ, 8, QF).astype(BF16)
        each(NJ, lambda d: c2(i, t, d, j_at(d), j).start())
        v[i, t, j] = q[i, t, j]

    def back(i, t):
        each(NJ, lambda d: c2(i, t, d, j_at(d), j_from(d)).wait_recv())
        return v[i, t].astype(F32).reshape(SLOTS, QF).astype(BF16)

    def gradients(i):
        slot_out = back(i, 0)
        mixed[i] = dot(clow[i], slot_out, 1, 0).astype(BF16)
        combine_grad = dot(cot[i], slot_out, 1, 1)
        combine = comb[i]
        part = combine * (combine_grad - jnp.sum(combine * combine_grad, axis=1, keepdims=True))
        in_grad = back(i, 1)
        dispatch_grad = dot(tok[i], in_grad, 1, 1)
        dispatch = disp[i]
        part += dispatch * (dispatch_grad - jnp.sum(dispatch * dispatch_grad, axis=0, keepdims=True))
        gp[i] = part
        d1(i).start()

    def gradients_across(i):
        d1(i).wait_recv()
        half = gp[i, mine] + ga[i]
        gzs[i] = half.astype(BF16)
        d2(i).start()
        ga[i] = half

    def gradients_whole(i):
        d2(i).wait_recv()
        half = ga[i] + gzr[i].astype(F32) + tcomb[i, mine]
        gf[i, mine] = half.astype(BF16).astype(F32)
        d3(i, mine).start()

    def finish(i):
        in_grad = v[i, 1].astype(F32).reshape(SLOTS, QF).astype(BF16)
        result = dot(dlow[i], in_grad, 1, 0)
        d3(i, theirs).wait_recv()
        tgrad[i] = (result + dot(gf[i].astype(BF16), sp[...], 1, 1)).astype(BF16)

    logits_send = [a1(i) for i in range(IMG)]
    for copy in logits_send:
        copy.start()
    logits_across(0)
    logits_across(1)
    logits_whole(0)
    softmaxes(0)
    logits_whole(1)
    softmaxes(1)
    to_experts(0)
    to_experts(1)
    arrive(0)
    w1_copy.wait()
    w2_copy.wait()
    expert(0)
    arrive(1)
    expert(1)
    to_images(0, 0)
    to_images(0, 1)
    gradients(0)
    gradients_across(0)
    to_images(1, 0)
    to_images(1, 1)
    gradients_whole(0)
    gradients(1)
    finish(0)
    gradients_across(1)
    gradients_whole(1)
    finish(1)

    for i in range(IMG):
        for copy in (a1(i), a2(i), a3(i, mine), d1(i), d2(i), d3(i, mine)):
            copy.wait_send()
        each(NJ, lambda d: b1(i, d, j_at(d), j).wait_send())
        each(NZ, lambda d: b2(i, d, z_at(d) % NZL, zh, zl).wait_send())
        each(NZ, lambda d: fwd(i, d, (z_at(NZ - d) // NZL) * 2 + c, z_at(NZ - d) % NZL).wait_send(), 0)
        for t in range(2):
            px(i, t).wait_send()
            each(NZ, lambda d: c1(i, t, d, z_at(d) // NZL, z_at(d) % NZL, zh, zl).wait_send())
            each(NJ, lambda d: c2(i, t, d, j_at(d), j).wait_send())


def per_device(tokens, slot_params, weight_in, bias_in, weight_out, bias_out, cotangent):
    vmem = pl.BlockSpec(memory_space=pltpu.VMEM)
    hbm = pl.BlockSpec(memory_space=pl.ANY)
    dma = pltpu.SemaphoreType.DMA
    pad = ((0, 0), (0, TP - TOK), (0, 0))
    scratch = [
        ((1024, 1024), BF16),
        ((1024, 1024), BF16),
        dma((2,)),
        ((IMG, TP, SLOTS), F32),
        ((IMG, HALF, SLOTS), F32),
        ((IMG, HALF, SLOTS), F32),
        ((IMG, HALF, SLOTS), F32),
        ((IMG, TP, SLOTS), F32),
        ((IMG, TP, SLOTS), F32),
        ((IMG, TP, SLOTS), F32),
        ((IMG, TP, SLOTS), F32),
        ((IMG, TP, SLOTS), BF16),
        ((IMG, TP, SLOTS), BF16),
        ((IMG, 2, NJ, 8, QF), BF16),
        ((IMG, 2, NJ, 8, QF), BF16),
        ((2, 2, SLOTS, 128), F32),
        ((IMG, NZL, 2, NJ, QF), BF16),
        ((IMG, 4, NZL, 2, NJ, QF), BF16),
        ((2, SLOTS, 1024), BF16),
        ((SLOTS, 1024), F32),
        ((IMG, 2, 2, SLOTS, QF), BF16),
        ((IMG, 2, 2, SLOTS, QF), BF16),
        ((IMG, 2, 2, NZL, NJ, QF), BF16),
        ((IMG, 2, 2, NZL, NJ, QF), BF16),
        ((2, 2, SLOTS, 128), F32),
        ((IMG, 2, NJ, 8, QF), BF16),
        ((IMG, 2, NJ, 8, QF), BF16),
        ((IMG, TP, SLOTS), F32),
        ((IMG, HALF, SLOTS), F32),
        ((IMG, HALF, SLOTS), BF16),
        ((IMG, HALF, SLOTS), BF16),
        ((IMG, TP, SLOTS), F32),
    ]
    scratch = [pltpu.VMEM(*a) if isinstance(a, tuple) else a for a in scratch]
    scratch += [dma((IMG,))] * 6 + [dma((IMG, NJ))] * 2 + [dma((IMG, NZ))] * 4 + [dma((IMG, 2))] * 2
    scratch += [dma((IMG, 2, NZ))] * 2 + [dma((IMG, 2, NJ))] * 2 + [dma((IMG,))] * 6
    mixed, token_grad, zloss = pl.pallas_call(
        kernel,
        out_shape=(
            jax.ShapeDtypeStruct((IMG, TP, QF), BF16),
            jax.ShapeDtypeStruct((IMG, TP, QF), BF16),
            jax.ShapeDtypeStruct((IMG, 8, TP), F32),
        ),
        in_specs=[vmem, vmem, hbm, vmem, hbm, vmem, vmem],
        out_specs=(vmem, vmem, vmem),
        scratch_shapes=scratch,
        compiler_params=pltpu.CompilerParams(
            collective_id=1, has_side_effects=True, vmem_limit_bytes=56 * 2**20
        ),
        name="layer",
    )(
        jnp.pad(tokens, pad),
        slot_params,
        weight_in.reshape(1024, 1024),
        bias_in,
        weight_out.reshape(1024, 1024),
        bias_out,
        jnp.pad(cotangent, pad),
    )
    return mixed[:, :TOK], token_grad[:, :TOK], zloss[:, 0, :TOK]


def solution(mesh):
    return jax.shard_map(
        per_device,
        mesh=mesh,
        in_specs=(
            P("expert", None, "hidden"),
            P("hidden", None),
            P("expert", None, "hidden"),
            P("expert", "hidden"),
            P("expert", "hidden", None),
            P("expert", "hidden"),
            P("expert", None, "hidden"),
        ),
        out_specs=(P("expert", None, "hidden"), P("expert", None, "hidden"), P("expert", None)),
        check_vma=False,
    )
```

```python
import jax
import jax.numpy as jnp
from jax import lax
from jax.experimental import pallas as pl
from jax.experimental.pallas import tpu as pltpu
from jax.sharding import PartitionSpec as P

loss_weight = 0.1
MESH = pl.DeviceIdType.MESH
F32, BF16 = jnp.float32, jnp.bfloat16

IMG, TOK, TP, HALF, QF, SLOTS = 2, 196, 208, 104, 256, 128
NJ, NZ, NZL = 16, 16, 8


def gelu_parts(value):
    factor = 0.7978845608028654
    inner = factor * (value + 0.044715 * value * value * value)
    slope_tanh = jnp.tanh(inner)
    result = 0.5 * value * (1.0 + slope_tanh)
    slope = 0.5 * (1.0 + slope_tanh) + 0.5 * value * (1.0 - slope_tanh * slope_tanh) * factor * (
        1.0 + 3.0 * 0.044715 * value * value
    )
    return result, slope


def dot(a, b, ca, cb):
    return lax.dot_general(a, b, (((ca,), (cb,)), ((), ())), preferred_element_type=F32)


def kernel(
    tok_in, sp, w1_hbm, bi, w2_hbm, bo, cot_in,
    mixed, tgrad, zloss,
    w1, w2, wsem, tok, cot,
    lp, la, lzs, lzr, lf,
    disp, comb, tcomb, dlow, clow,
    s, r1, fa, r2, x,
    act, slope, px_s, px_r, cs, y, fb, q, v,
    gp, ga, gzs, gzr, gf,
    a1s, a1r, a2s, a2r, a3s, a3r, b1s, b1r, b2s, b2r, fws, fwr,
    pxs, pxr, c1s, c1r, c2s, c2r, d1s, d1r, d2s, d2r, d3s, d3r,
):
    div, rem = lax.div, lax.rem
    e, h = lax.axis_index("expert"), lax.axis_index("hidden")
    j, zl, zh, c = div(e, NZL), rem(e, NZL), div(h, 2), rem(h, 2)
    jy, jx = div(j, 4), rem(j, 4)
    z = zh * NZL + zl
    core_peer = (e, zh * 2 + 1 - c)
    z8_peer = (e, (1 - zh) * 2 + c)

    def z_at(d):
        zz = rem(z + d, NZ)
        return div(zz, NZL), rem(zz, NZL)

    def z_dev(place):
        return (j * NZL + place[1], place[0] * 2 + c)

    def j_at(d):
        return rem(jy + div(d, 4), 4) * 4 + rem(jx + rem(d, 4), 4)

    def j_dev(jj):
        return (jj * NZL + zl, h)

    def rc(src, dst, ss, rs, dev):
        return pltpu.make_async_remote_copy(
            src_ref=src, dst_ref=dst, send_sem=ss, recv_sem=rs, device_id=dev, device_id_type=MESH
        )

    def each(n, body, start=1):
        lax.fori_loop(start, n, lambda k, carry: (body(k), carry)[1], 0)

    def far_first(k):
        return lax.select(rem(k, 2) == 1, 8 + div(k, 2), 8 - div(k, 2))

    barrier = pltpu.get_barrier_semaphore()
    pl.semaphore_signal(barrier, inc=1, device_id=core_peer, device_id_type=MESH)
    each(
        NZ,
        lambda k: pl.semaphore_signal(barrier, inc=1, device_id=z_dev(z_at(far_first(k))), device_id_type=MESH),
    )
    each(NJ, lambda d: pl.semaphore_signal(barrier, inc=1, device_id=j_dev(j_at(d)), device_id_type=MESH))
    w1_copy = pltpu.make_async_copy(w1_hbm, w1, wsem.at[0])
    w2_copy = pltpu.make_async_copy(w2_hbm, w2, wsem.at[1])
    w1_copy.start()
    w2_copy.start()

    mine, theirs = pl.ds(pl.multiple_of(c * HALF, 8), HALF), pl.ds(pl.multiple_of((1 - c) * HALF, 8), HALF)

    def laid_out(given, kept):
        for i in range(IMG):
            kept[i, TP - 16 : TP, :] = jnp.zeros((16, QF), BF16)
        whole = given[...].astype(F32)
        for i in range(IMG):
            kept[i, 0:TOK, :] = whole[:, i, :].astype(BF16)

    laid_out(tok_in, tok)
    for i in range(IMG):
        lp[i] = dot(tok[i], sp[...], 1, 0)
    pl.semaphore_wait(barrier, 1 + (NZ - 1) + (NJ - 1))

    def a1(i):
        return rc(lp.at[i, theirs], la.at[i], a1s.at[i], a1r.at[i], core_peer)

    def a2(i):
        return rc(lzs.at[i], lzr.at[i], a2s.at[i], a2r.at[i], z8_peer)

    def a3(i, rows):
        return rc(lf.at[i, rows], lf.at[i, rows], a3s.at[i], a3r.at[i], core_peer)

    def b1(i, t, src, dst, dev):
        return rc(s.at[i, t, src], r1.at[i, t, dst], b1s.at[i, t], b1r.at[i, t], dev)

    def b2(i, t, place):
        return rc(
            r2.at[i, t, place[1]], x.at[i, t, (zh * 2 + c) * NZL + zl], b2s.at[i, t], b2r.at[i, t], z_dev(place)
        )

    def fwd(i, t, half, core):
        there = x.at[i, t, pl.ds((half * 2 + core) * NZL, NZL)]
        return rc(there, there, fws.at[i, t, half], fwr.at[i, t, half], core_peer)

    def px(i, t):
        return rc(px_s.at[i, t], px_r.at[i, t], pxs.at[i, t], pxr.at[i, t], core_peer)

    def c1(i, t, place):
        return rc(cs.at[i, t, place[0] * NZL + place[1]], y.at[i, t, z], c1s.at[i, t], c1r.at[i, t], z_dev(place))

    def c2(i, t, dst, dev):
        return rc(q.at[i, t, dst], v.at[i, t, j], c2s.at[i, t], c2r.at[i, t], dev)

    fifteen = pl.ds(0, 15)

    def b1_all(i, t):
        return rc(s.at[i, t, fifteen], r1.at[i, t, fifteen], b1s.at[i, t], b1r.at[i, t], core_peer)

    def b2_all(i, t):
        return rc(x.at[i, t, fifteen], x.at[i, t, fifteen], b2s.at[i, t], b2r.at[i, t], core_peer)

    def c1_all(i, t):
        return rc(cs.at[i, t, fifteen], y.at[i, t, fifteen], c1s.at[i, t], c1r.at[i, t], core_peer)

    def c2_all(i, t):
        return rc(q.at[i, t, fifteen], v.at[i, t, fifteen], c2s.at[i, t], c2r.at[i, t], core_peer)

    def d1(i):
        return rc(gp.at[i, theirs], ga.at[i], d1s.at[i], d1r.at[i], core_peer)

    def d2(i):
        return rc(gzs.at[i], gzr.at[i], d2s.at[i], d2r.at[i], z8_peer)

    def d3(i, rows):
        return rc(gf.at[i, rows], gf.at[i, rows], d3s.at[i], d3r.at[i], core_peer)

    def logits_across(i):
        a1(i).wait_recv()
        lzs[i] = lp[i, mine] + la[i]
        a2(i).start()

    def logits_whole(i):
        a2(i).wait_recv()
        lf[i, mine] = lzs[i] + lzr[i]
        a3(i, mine).start()

    def send_slots(i, t):
        each(NJ, lambda d: b1(i, t, j_at(d), j, j_dev(j_at(d))).start())
        r1[i, t, j] = s[i, t, j]

    def dispatches(i):
        a3(i, theirs).wait_recv()
        row = lax.broadcasted_iota(jnp.int32, (TP, SLOTS), 0)
        masked = jnp.where(row < TOK, lf[i], -1e30)
        top = jnp.max(masked, axis=0, keepdims=True)
        up = jnp.exp(masked - top)
        dispatch = up / jnp.sum(up, axis=0, keepdims=True)
        disp[i] = dispatch
        dispatch_low = dispatch.astype(BF16)
        dlow[i] = dispatch_low
        s[i, 0] = dot(dispatch_low, tok[i], 0, 0).reshape(NJ, 8, QF).astype(BF16)
        send_slots(i, 0)

    def combines(i):
        logits = lf[i]
        top = jnp.max(logits, axis=1, keepdims=True)
        up = jnp.exp(logits - top)
        below = jnp.sum(up, axis=1, keepdims=True)
        combine = up / below
        comb[i] = combine
        combine_low = combine.astype(BF16)
        clow[i] = combine_low
        s[i, 1] = dot(combine_low, cot[i], 0, 0).reshape(NJ, 8, QF).astype(BF16)
        send_slots(i, 1)
        total = top + jnp.log(below)
        tcomb[i] = (2.0 * loss_weight) * total * combine
        wide = jnp.broadcast_to(loss_weight * total * total, (TP, SLOTS))
        zloss[i : i + 1, :] = jnp.transpose(wide)[0:1, 0:TOK]

    def to_experts(i, t):
        b1_all(i, t).wait_recv()
        rows = r1[i, t].astype(F32).reshape(SLOTS, QF)
        for lanes in range(2):
            fa[t, lanes] = rows[:, lanes * 128 : (lanes + 1) * 128]
        for low in range(NZL):
            rows = [fa[t, lanes, pl.ds(low, NJ, stride=8), :] for lanes in range(2)]
            r2[i, t, low] = jnp.concatenate(rows, axis=1).astype(BF16)
        each(NZ, lambda k: b2(i, t, z_at(far_first(k))).start())
        x[i, t, h * NZL + zl] = r2[i, t, zl]

    def arrive(i, t):
        b2_all(i, t).wait_recv()
        for half in range(2):
            fwd(i, t, half, c).start()

    def rows_of(i, t):
        for half in range(2):
            fwd(i, t, half, 1 - c).wait_recv()
        return jnp.concatenate(
            [x[i, t, k * NZL : (k + 1) * NZL].reshape(SLOTS, QF) for k in range(4)], axis=1
        )

    def quarter(k, core):
        return pl.ds(pl.multiple_of((k * 2 + core) * QF, QF), QF)

    FB = 256

    def expert_out(i):
        arrived = rows_of(i, 0)
        for f in range(0, 1024, FB):
            part = dot(arrived, w1[:, f : f + FB], 1, 0) + bi[:, f : f + FB].astype(F32)
            activated, slope_part = gelu_parts(part)
            act[0, :, f : f + FB] = activated.astype(BF16)
            slope[:, f : f + FB] = slope_part
        send_results(i, 0, lambda cols: dot(act[0], w2[:, cols], 1, 0))

    def expert_grad(i):
        arrived = rows_of(i, 1)
        for f in range(0, 1024, FB):
            part = dot(arrived, w2[f : f + FB, :], 1, 1) * slope[:, f : f + FB]
            act[1, :, f : f + FB] = part.astype(BF16)
        send_results(i, 1, lambda cols: dot(act[1], w1[cols, :], 1, 1))

    def send_results(i, t, product):
        for k in range(2):
            px_s[i, t, k] = product(quarter(k, 1 - c)).astype(BF16)
        px(i, t).start()
        own = [product(quarter(k, c)) for k in range(2)]
        px(i, t).wait_recv()
        for k in range(2):
            total = own[k] + px_r[i, t, k].astype(F32)
            if t == 0:
                total = total + jnp.where(zh == k, 1.0, 0.0) * bo[...].astype(F32)
            cs[i, t, k * NZL : (k + 1) * NZL] = total.reshape(NZL, NJ, QF).astype(BF16)
        each(NZ, lambda k: c1(i, t, z_at(far_first(k))).start())
        y[i, t, z] = cs[i, t, z]

    def to_images(i, t):
        c1_all(i, t).wait_recv()
        for low in range(NZL):
            rows = y[i, t, low].astype(F32) + y[i, t, NZL + low].astype(F32)
            for lanes in range(2):
                fb[t, lanes, pl.ds(low, NJ, stride=8), :] = rows[:, lanes * 128 : (lanes + 1) * 128]
        rows = jnp.concatenate([fb[t, lanes] for lanes in range(2)], axis=1)
        q[i, t] = rows.reshape(NJ, 8, QF).astype(BF16)
        each(NJ, lambda d: c2(i, t, j_at(d), j_dev(j_at(d))).start())
        v[i, t, j] = q[i, t, j]

    def back(i, t):
        return v[i, t].astype(F32).reshape(SLOTS, QF).astype(BF16)

    def outputs(i):
        c2_all(i, 0).wait_recv()
        slot_out = back(i, 0)
        mixed[i] = dot(clow[i], slot_out, 1, 0).astype(BF16)[0:TOK, :]
        combine_grad = dot(cot[i], slot_out, 1, 1)
        combine = comb[i]
        gp[i] = combine * (combine_grad - jnp.sum(combine * combine_grad, axis=1, keepdims=True))

    def gradients(i):
        c2_all(i, 1).wait_recv()
        dispatch_grad = dot(tok[i], back(i, 1), 1, 1)
        dispatch = disp[i]
        gp[i] += dispatch * (dispatch_grad - jnp.sum(dispatch * dispatch_grad, axis=0, keepdims=True))
        d1(i).start()

    def gradients_across(i):
        d1(i).wait_recv()
        half = gp[i, mine] + ga[i]
        gzs[i] = half.astype(BF16)
        d2(i).start()
        ga[i] = half + tcomb[i, mine]

    def gradients_whole(i):
        d2(i).wait_recv()
        half = ga[i] + gzr[i].astype(F32)
        gf[i, mine] = half.astype(BF16).astype(F32)
        d3(i, mine).start()

    def finish(i):
        result = dot(dlow[i], back(i, 1), 1, 0)
        d3(i, theirs).wait_recv()
        tgrad[i] = (result + dot(gf[i].astype(BF16), sp[...], 1, 1)).astype(BF16)[0:TOK, :]

    for copy in [a1(i) for i in range(IMG)]:
        copy.start()
    logits_across(0)
    logits_across(1)
    laid_out(cot_in, cot)
    logits_whole(0)
    dispatches(0)
    combines(0)
    logits_whole(1)
    to_experts(0, 0)
    to_experts(0, 1)
    dispatches(1)
    combines(1)
    to_experts(1, 0)
    to_experts(1, 1)
    w1_copy.wait()
    w2_copy.wait()
    arrive(0, 0)
    expert_out(0)
    arrive(0, 1)
    expert_grad(0)
    arrive(1, 0)
    expert_out(1)
    arrive(1, 1)
    expert_grad(1)
    to_images(0, 0)
    to_images(0, 1)
    outputs(0)
    gradients(0)
    gradients_across(0)
    to_images(1, 0)
    to_images(1, 1)
    outputs(1)
    gradients_whole(0)
    gradients(1)
    finish(0)
    gradients_across(1)
    gradients_whole(1)
    finish(1)

    for i in range(IMG):
        for copy in (a1(i), a2(i), a3(i, mine), d1(i), d2(i), d3(i, mine)):
            copy.wait_send()
        for t in range(2):
            for copy in (b1_all(i, t), b2_all(i, t), fwd(i, t, 0, c), fwd(i, t, 1, c)):
                copy.wait_send()
            for copy in (px(i, t), c1_all(i, t), c2_all(i, t)):
                copy.wait_send()


def per_device(tokens, slot_params, weight_in, bias_in, weight_out, bias_out, cotangent):
    vmem = pl.BlockSpec(memory_space=pltpu.VMEM)
    hbm = pl.BlockSpec(memory_space=pl.ANY)
    dma = pltpu.SemaphoreType.DMA
    scratch = [
        ((1024, 1024), BF16),
        ((1024, 1024), BF16),
        dma((2,)),
        ((IMG, TP, QF), BF16),
        ((IMG, TP, QF), BF16),
        ((IMG, TP, SLOTS), F32),
        ((IMG, HALF, SLOTS), F32),
        ((IMG, HALF, SLOTS), F32),
        ((IMG, HALF, SLOTS), F32),
        ((IMG, TP, SLOTS), F32),
        ((IMG, TP, SLOTS), F32),
        ((IMG, TP, SLOTS), F32),
        ((IMG, TP, SLOTS), F32),
        ((IMG, TP, SLOTS), BF16),
        ((IMG, TP, SLOTS), BF16),
        ((IMG, 2, NJ, 8, QF), BF16),
        ((IMG, 2, NJ, 8, QF), BF16),
        ((2, 2, SLOTS, 128), F32),
        ((IMG, 2, NZL, NJ, QF), BF16),
        ((IMG, 2, 4 * NZL, NJ, QF), BF16),
        ((2, SLOTS, 1024), BF16),
        ((SLOTS, 1024), F32),
        ((IMG, 2, 2, SLOTS, QF), BF16),
        ((IMG, 2, 2, SLOTS, QF), BF16),
        ((IMG, 2, NZ, NJ, QF), BF16),
        ((IMG, 2, NZ, NJ, QF), BF16),
        ((2, 2, SLOTS, 128), F32),
        ((IMG, 2, NJ, 8, QF), BF16),
        ((IMG, 2, NJ, 8, QF), BF16),
        ((IMG, TP, SLOTS), F32),
        ((IMG, HALF, SLOTS), F32),
        ((IMG, HALF, SLOTS), BF16),
        ((IMG, HALF, SLOTS), BF16),
        ((IMG, TP, SLOTS), F32),
    ]
    scratch = [pltpu.VMEM(*a) if isinstance(a, tuple) else a for a in scratch]
    scratch += [dma((IMG,))] * 6 + [dma((IMG, 2))] * 4 + [dma((IMG, 2, 2))] * 2 + [dma((IMG, 2))] * 6 + [dma((IMG,))] * 6
    return pl.pallas_call(
        kernel,
        out_shape=(
            jax.ShapeDtypeStruct((IMG, TOK, QF), BF16),
            jax.ShapeDtypeStruct((IMG, TOK, QF), BF16),
            jax.ShapeDtypeStruct((IMG, TOK), F32),
        ),
        in_specs=[vmem, vmem, hbm, vmem, hbm, vmem, vmem],
        out_specs=(vmem, vmem, vmem),
        scratch_shapes=scratch,
        compiler_params=pltpu.CompilerParams(
            collective_id=1, has_side_effects=True, vmem_limit_bytes=56 * 2**20
        ),
        name="layer",
    )(
        jnp.transpose(tokens, (1, 0, 2)),
        slot_params,
        weight_in.reshape(1024, 1024),
        bias_in,
        weight_out.reshape(1024, 1024),
        bias_out,
        jnp.transpose(cotangent, (1, 0, 2)),
    )


def solution(mesh):
    return jax.shard_map(
        per_device,
        mesh=mesh,
        in_specs=(
            P("expert", None, "hidden"),
            P("hidden", None),
            P("expert", None, "hidden"),
            P("expert", "hidden"),
            P("expert", "hidden", None),
            P("expert", "hidden"),
            P("expert", None, "hidden"),
        ),
        out_specs=(P("expert", None, "hidden"), P("expert", None, "hidden"), P("expert", None)),
        check_vma=False,
    )
```

```python
import jax
import jax.numpy as jnp
from jax import lax
from jax.experimental import pallas as pl
from jax.experimental.pallas import tpu as pltpu
from jax.sharding import PartitionSpec as P

loss_weight = 0.1
MESH = pl.DeviceIdType.MESH
F32, BF16 = jnp.float32, jnp.bfloat16

IMG, TOK, TP, HALF, QF, SLOTS = 2, 196, 208, 104, 256, 128
NJ, NZ, NZL = 16, 16, 8


def gelu_parts(value):
    factor = 0.7978845608028654
    inner = factor * (value + 0.044715 * value * value * value)
    slope_tanh = jnp.tanh(inner)
    result = 0.5 * value * (1.0 + slope_tanh)
    slope = 0.5 * (1.0 + slope_tanh) + 0.5 * value * (1.0 - slope_tanh * slope_tanh) * factor * (
        1.0 + 3.0 * 0.044715 * value * value
    )
    return result, slope


def dot(a, b, ca, cb):
    return lax.dot_general(a, b, (((ca,), (cb,)), ((), ())), preferred_element_type=F32)


def kernel(
    tok_hbm, sp_hbm, w1_hbm, bi_hbm, w2_hbm, bo_hbm, cot_hbm,
    mixed, tgrad, zloss,
    tok_in, sp, w1, bi, w2, bo, cot_in, insem, tok, cot,
    lp, la, lzs, lzr, lf,
    disp, comb, tcomb, dlow, clow,
    s, r1, fa, r2, x,
    act, slope, part, px_s, px_r, ft, cq, cr, fc, cs, y, fb, v,
    gp, ga, gzs, gzr, gf,
    a1s, a1r, a2s, a2r, a3s, a3r, b1s, b1r, b2s, b2r, fws, fwr,
    pxs, pxr, c1s, c1r, c2s, c2r, d1s, d1r, d2s, d2r, d3s, d3r,
):
    div, rem = lax.div, lax.rem
    e, h = lax.axis_index("expert"), lax.axis_index("hidden")
    j, zl, zh, c = div(e, NZL), rem(e, NZL), div(h, 2), rem(h, 2)
    jy, jx = div(j, 4), rem(j, 4)
    z = zh * NZL + zl
    core_peer = (e, zh * 2 + 1 - c)
    z8_peer = (e, (1 - zh) * 2 + c)

    def z_at(d):
        zz = rem(z + d, NZ)
        return div(zz, NZL), rem(zz, NZL)

    def z_dev(place):
        return (j * NZL + place[1], place[0] * 2 + c)

    def j_at(d):
        return rem(jy + div(d, 4), 4) * 4 + rem(jx + rem(d, 4), 4)

    def j_dev(jj):
        return (jj * NZL + zl, h)

    def rc(src, dst, ss, rs, dev):
        return pltpu.make_async_remote_copy(
            src_ref=src, dst_ref=dst, send_sem=ss, recv_sem=rs, device_id=dev, device_id_type=MESH
        )

    def each(n, body, start=1):
        lax.fori_loop(start, n, lambda k, carry: (body(k), carry)[1], 0)

    def far_first(k):
        return lax.select(rem(k, 2) == 1, 8 + div(k, 2), 8 - div(k, 2))

    barrier = pltpu.get_barrier_semaphore()
    pl.semaphore_signal(barrier, inc=1, device_id=core_peer, device_id_type=MESH)
    each(
        NZ,
        lambda k: pl.semaphore_signal(barrier, inc=1, device_id=z_dev(z_at(far_first(k))), device_id_type=MESH),
    )
    each(NJ, lambda d: pl.semaphore_signal(barrier, inc=1, device_id=j_dev(j_at(d)), device_id_type=MESH))
    given = (tok_hbm, sp_hbm, cot_hbm, w1_hbm, bi_hbm, w2_hbm, bo_hbm)
    kept = (tok_in, sp, cot_in, w1, bi, w2, bo)
    loads = [pltpu.make_async_copy(a, b, insem.at[k]) for k, (a, b) in enumerate(zip(given, kept))]
    for load in loads:
        load.start()

    mine, theirs = pl.ds(pl.multiple_of(c * HALF, 8), HALF), pl.ds(pl.multiple_of((1 - c) * HALF, 8), HALF)

    def laid_out(given, kept):
        for i in range(IMG):
            kept[i, TP - 16 : TP, :] = jnp.zeros((16, QF), BF16)
        whole = given[...].astype(F32)
        for i in range(IMG):
            kept[i, 0:TOK, :] = whole[:, i, :].astype(BF16)

    loads[0].wait()
    laid_out(tok_in, tok)
    loads[1].wait()
    for i in range(IMG):
        lp[i] = dot(tok[i], sp[...], 1, 0)
    pl.semaphore_wait(barrier, 1 + (NZ - 1) + (NJ - 1))

    def a1(i):
        return rc(lp.at[i, theirs], la.at[i], a1s.at[i], a1r.at[i], core_peer)

    def a2(i):
        return rc(lzs.at[i], lzr.at[i], a2s.at[i], a2r.at[i], z8_peer)

    def a3(i, rows):
        return rc(lf.at[i, rows], lf.at[i, rows], a3s.at[i], a3r.at[i], core_peer)

    def b1(i, t, src, dst, dev):
        return rc(s.at[i, t, src], r1.at[i, t, dst], b1s.at[i, t], b1r.at[i, t], dev)

    def b2(i, t, place):
        return rc(
            r2.at[i, t, place[1]], x.at[i, t, (zh * 2 + c) * NZL + zl], b2s.at[i, t], b2r.at[i, t], z_dev(place)
        )

    def fwd(i, t, half, core):
        there = x.at[i, t, pl.ds((half * 2 + core) * NZL, NZL)]
        return rc(there, there, fws.at[i, t, half], fwr.at[i, t, half], core_peer)

    def px(i, t):
        return rc(px_s.at[i, t], px_r.at[i, t], pxs.at[i, t], pxr.at[i, t], core_peer)

    def c1(i, t, dst, dev):
        return rc(cq.at[i, t, dst], cr.at[i, t, j], c1s.at[i, t], c1r.at[i, t], dev)

    def c2(i, t, place):
        return rc(cs.at[i, t, place[0] * NZL + place[1]], y.at[i, t, z], c2s.at[i, t], c2r.at[i, t], z_dev(place))

    fifteen = pl.ds(0, 15)

    def b1_all(i, t):
        return rc(s.at[i, t, fifteen], r1.at[i, t, fifteen], b1s.at[i, t], b1r.at[i, t], core_peer)

    def b2_all(i, t):
        return rc(x.at[i, t, fifteen], x.at[i, t, fifteen], b2s.at[i, t], b2r.at[i, t], core_peer)

    def c1_all(i, t):
        return rc(cq.at[i, t, fifteen], cr.at[i, t, fifteen], c1s.at[i, t], c1r.at[i, t], core_peer)

    def c2_all(i, t):
        return rc(cs.at[i, t, fifteen], y.at[i, t, fifteen], c2s.at[i, t], c2r.at[i, t], core_peer)

    def d1(i):
        return rc(gp.at[i, theirs], ga.at[i], d1s.at[i], d1r.at[i], core_peer)

    def d2(i):
        return rc(gzs.at[i], gzr.at[i], d2s.at[i], d2r.at[i], z8_peer)

    def d3(i, rows):
        return rc(gf.at[i, rows], gf.at[i, rows], d3s.at[i], d3r.at[i], core_peer)

    def logits_across(i):
        a1(i).wait_recv()
        lzs[i] = lp[i, mine] + la[i]
        a2(i).start()

    def logits_whole(i):
        a2(i).wait_recv()
        lf[i, mine] = lzs[i] + lzr[i]
        a3(i, mine).start()

    def send_slots(i, t):
        each(NJ, lambda d: b1(i, t, j_at(d), j, j_dev(j_at(d))).start())
        r1[i, t, j] = s[i, t, j]

    def dispatches(i):
        a3(i, theirs).wait_recv()
        row = lax.broadcasted_iota(jnp.int32, (TP, SLOTS), 0)
        masked = jnp.where(row < TOK, lf[i], -1e30)
        top = jnp.max(masked, axis=0, keepdims=True)
        up = jnp.exp(masked - top)
        dispatch = up / jnp.sum(up, axis=0, keepdims=True)
        disp[i] = dispatch
        dispatch_low = dispatch.astype(BF16)
        dlow[i] = dispatch_low
        s[i, 0] = dot(dispatch_low, tok[i], 0, 0).reshape(NJ, 8, QF).astype(BF16)
        send_slots(i, 0)

    def combines(i):
        logits = lf[i]
        top = jnp.max(logits, axis=1, keepdims=True)
        up = jnp.exp(logits - top)
        below = jnp.sum(up, axis=1, keepdims=True)
        combine = up / below
        comb[i] = combine
        combine_low = combine.astype(BF16)
        clow[i] = combine_low
        s[i, 1] = dot(combine_low, cot[i], 0, 0).reshape(NJ, 8, QF).astype(BF16)
        send_slots(i, 1)
        total = top + jnp.log(below)
        tcomb[i] = (2.0 * loss_weight) * total * combine
        wide = jnp.broadcast_to(loss_weight * total * total, (TP, SLOTS))
        zloss[i : i + 1, :] = jnp.transpose(wide)[0:1, 0:TOK]

    def to_experts(i, t):
        b1_all(i, t).wait_recv()
        rows = r1[i, t].astype(F32).reshape(SLOTS, QF)
        for lanes in range(2):
            fa[t, lanes] = rows[:, lanes * 128 : (lanes + 1) * 128]
        for low in range(NZL):
            rows = [fa[t, lanes, pl.ds(low, NJ, stride=8), :] for lanes in range(2)]
            r2[i, t, low] = jnp.concatenate(rows, axis=1).astype(BF16)
        each(NZ, lambda k: b2(i, t, z_at(far_first(k))).start())
        x[i, t, h * NZL + zl] = r2[i, t, zl]

    def arrive(i, t):
        b2_all(i, t).wait_recv()
        for half in range(2):
            fwd(i, t, half, c).start()

    def quarter(k, core):
        return pl.ds(pl.multiple_of((k * 2 + core) * QF, QF), QF)

    FB = 256

    def by_features(i, t, core, product):
        arrived = [x[i, t, pl.ds((k * 2 + core) * NZL, NZL)].reshape(SLOTS, QF) for k in range(2)]
        for f in range(0, 1024, FB):
            yield f, sum(product(arrived[k], quarter(k, core), f) for k in range(2))

    def project(i, t, product):
        for f, total in by_features(i, t, c, product):
            part[:, f : f + FB] = total
        for half in range(2):
            fwd(i, t, half, 1 - c).wait_recv()
        for f, total in by_features(i, t, 1 - c, product):
            yield f, part[:, f : f + FB] + total

    def expert_out(i):
        def product(rows, features, f):
            return dot(rows, w1[features, f : f + FB], 1, 0)

        for f, total in project(i, 0, product):
            activated, slope_part = gelu_parts(total + bi[:, f : f + FB].astype(F32))
            act[0, :, f : f + FB] = activated.astype(BF16)
            slope[:, f : f + FB] = slope_part
        send_results(i, 0, lambda cols: dot(act[0], w2[:, cols], 1, 0))

    def expert_grad(i):
        def product(rows, features, f):
            return dot(rows, w2[f : f + FB, features], 1, 1)

        for f, total in project(i, 1, product):
            act[1, :, f : f + FB] = (total * slope[:, f : f + FB]).astype(BF16)
        send_results(i, 1, lambda cols: dot(act[1], w1[cols, :], 1, 1))

    def send_results(i, t, product):
        for k in range(2):
            px_s[i, t, k] = product(quarter(k, 1 - c)).astype(BF16)
        px(i, t).start()
        own = [product(quarter(k, c)) for k in range(2)]
        px(i, t).wait_recv()
        for k in range(2):
            total = own[k] + px_r[i, t, k].astype(F32)
            if t == 0:
                total = total + jnp.where(zh == k, 1.0, 0.0) * bo[...].astype(F32)
            for lanes in range(2):
                ft[k, lanes] = total[:, lanes * 128 : (lanes + 1) * 128]
        for dst in range(NJ):
            for k in range(2):
                rows = [ft[k, lanes, pl.ds(dst, 8, stride=NJ), :] for lanes in range(2)]
                cq[i, t, dst, k] = jnp.concatenate(rows, axis=1).astype(BF16)
        each(NJ, lambda d: c1(i, t, j_at(d), j_dev(j_at(d))).start())
        cr[i, t, j] = cq[i, t, j]

    def turn(i, t):
        c1_all(i, t).wait_recv()
        for k in range(2):
            rows = cr[i, t, :, k].astype(F32).reshape(SLOTS, QF)
            for lanes in range(2):
                fc[k, lanes] = rows[:, lanes * 128 : (lanes + 1) * 128]
        for k in range(2):
            for low in range(NZL):
                rows = [fc[k, lanes, pl.ds(low, NJ, stride=8), :] for lanes in range(2)]
                cs[i, t, k * NZL + low] = jnp.concatenate(rows, axis=1).astype(BF16)
        each(NZ, lambda k: c2(i, t, z_at(far_first(k))).start())
        y[i, t, z] = cs[i, t, z]

    def home(i, t):
        c2_all(i, t).wait_recv()
        for low in range(NZL):
            rows = y[i, t, low].astype(F32) + y[i, t, NZL + low].astype(F32)
            for lanes in range(2):
                fb[lanes, pl.ds(low, NJ, stride=8), :] = rows[:, lanes * 128 : (lanes + 1) * 128]
        v[i, t] = jnp.concatenate([fb[lanes] for lanes in range(2)], axis=1).astype(BF16)

    def outputs(i):
        slot_out = v[i, 0]
        mixed[i] = dot(clow[i], slot_out, 1, 0).astype(BF16)[0:TOK, :]
        combine_grad = dot(cot[i], slot_out, 1, 1)
        combine = comb[i]
        gp[i] = combine * (combine_grad - jnp.sum(combine * combine_grad, axis=1, keepdims=True))

    def gradients(i):
        dispatch_grad = dot(tok[i], v[i, 1], 1, 1)
        dispatch = disp[i]
        gp[i] += dispatch * (dispatch_grad - jnp.sum(dispatch * dispatch_grad, axis=0, keepdims=True))
        d1(i).start()

    def gradients_across(i):
        d1(i).wait_recv()
        half = gp[i, mine] + ga[i]
        gzs[i] = half.astype(BF16)
        d2(i).start()
        ga[i] = half + tcomb[i, mine]

    def gradients_whole(i):
        d2(i).wait_recv()
        half = ga[i] + gzr[i].astype(F32)
        gf[i, mine] = half.astype(BF16).astype(F32)
        d3(i, mine).start()

    def finish(i):
        result = dot(dlow[i], v[i, 1], 1, 0)
        d3(i, theirs).wait_recv()
        tgrad[i] = (result + dot(gf[i].astype(BF16), sp[...], 1, 1)).astype(BF16)[0:TOK, :]

    for copy in [a1(i) for i in range(IMG)]:
        copy.start()
    logits_across(0)
    logits_across(1)
    loads[2].wait()
    laid_out(cot_in, cot)
    logits_whole(0)
    dispatches(0)
    combines(0)
    logits_whole(1)
    to_experts(0, 0)
    to_experts(0, 1)
    dispatches(1)
    combines(1)
    to_experts(1, 0)
    to_experts(1, 1)
    for load in loads[3:]:
        load.wait()
    arrive(0, 0)
    expert_out(0)
    arrive(0, 1)
    expert_grad(0)
    turn(0, 0)
    arrive(1, 0)
    expert_out(1)
    turn(0, 1)
    arrive(1, 1)
    expert_grad(1)
    turn(1, 0)
    turn(1, 1)
    home(0, 0)
    outputs(0)
    home(0, 1)
    gradients(0)
    gradients_across(0)
    home(1, 0)
    outputs(1)
    home(1, 1)
    gradients(1)
    gradients_across(1)
    gradients_whole(0)
    finish(0)
    for i in range(IMG):
        for copy in (a1(i), a2(i), a3(i, mine), d1(i), d2(i)):
            copy.wait_send()
        for t in range(2):
            for copy in (b1_all(i, t), b2_all(i, t), fwd(i, t, 0, c), fwd(i, t, 1, c)):
                copy.wait_send()
            for copy in (px(i, t), c1_all(i, t), c2_all(i, t)):
                copy.wait_send()
    gradients_whole(1)
    finish(1)
    d3(0, mine).wait_send()
    d3(1, mine).wait_send()


def per_device(tokens, slot_params, weight_in, bias_in, weight_out, bias_out, cotangent):
    vmem = pl.BlockSpec(memory_space=pltpu.VMEM)
    hbm = pl.BlockSpec(memory_space=pltpu.HBM)
    dma = pltpu.SemaphoreType.DMA
    scratch = [
        ((TOK, IMG, QF), BF16),
        ((QF, SLOTS), BF16),
        ((1024, 1024), BF16),
        ((1, 1024), BF16),
        ((1024, 1024), BF16),
        ((1, QF), BF16),
        ((TOK, IMG, QF), BF16),
        dma((7,)),
        ((IMG, TP, QF), BF16),
        ((IMG, TP, QF), BF16),
        ((IMG, TP, SLOTS), F32),
        ((IMG, HALF, SLOTS), F32),
        ((IMG, HALF, SLOTS), F32),
        ((IMG, HALF, SLOTS), F32),
        ((IMG, TP, SLOTS), F32),
        ((IMG, TP, SLOTS), F32),
        ((IMG, TP, SLOTS), F32),
        ((IMG, TP, SLOTS), F32),
        ((IMG, TP, SLOTS), BF16),
        ((IMG, TP, SLOTS), BF16),
        ((IMG, 2, NJ, 8, QF), BF16),
        ((IMG, 2, NJ, 8, QF), BF16),
        ((2, 2, SLOTS, 128), F32),
        ((IMG, 2, NZL, NJ, QF), BF16),
        ((IMG, 2, 4 * NZL, NJ, QF), BF16),
        ((2, SLOTS, 1024), BF16),
        ((SLOTS, 1024), F32),
        ((SLOTS, 1024), F32),
        ((IMG, 2, 2, SLOTS, QF), BF16),
        ((IMG, 2, 2, SLOTS, QF), BF16),
        ((2, 2, SLOTS, 128), F32),
        ((IMG, 2, NJ, 2, 8, QF), BF16),
        ((IMG, 2, NJ, 2, 8, QF), BF16),
        ((2, 2, SLOTS, 128), F32),
        ((IMG, 2, NZ, NJ, QF), BF16),
        ((IMG, 2, NZ, NJ, QF), BF16),
        ((2, SLOTS, 128), F32),
        ((IMG, 2, SLOTS, QF), BF16),
        ((IMG, TP, SLOTS), F32),
        ((IMG, HALF, SLOTS), F32),
        ((IMG, HALF, SLOTS), BF16),
        ((IMG, HALF, SLOTS), BF16),
        ((IMG, TP, SLOTS), F32),
    ]
    scratch = [pltpu.VMEM(*a) if isinstance(a, tuple) else a for a in scratch]
    scratch += [dma((IMG,))] * 6 + [dma((IMG, 2))] * 4 + [dma((IMG, 2, 2))] * 2 + [dma((IMG, 2))] * 6 + [dma((IMG,))] * 6
    return pl.pallas_call(
        kernel,
        out_shape=(
            jax.ShapeDtypeStruct((IMG, TOK, QF), BF16),
            jax.ShapeDtypeStruct((IMG, TOK, QF), BF16),
            jax.ShapeDtypeStruct((IMG, TOK), F32),
        ),
        in_specs=[hbm] * 7,
        out_specs=(vmem, vmem, vmem),
        scratch_shapes=scratch,
        compiler_params=pltpu.CompilerParams(
            collective_id=1, has_side_effects=True, vmem_limit_bytes=20 * 2**20
        ),
        name="layer",
    )(
        *(
            pltpu.with_memory_space_constraint(given, pltpu.HBM)
            for given in (
                jnp.transpose(tokens, (1, 0, 2)),
                slot_params,
                weight_in.reshape(1024, 1024),
                bias_in,
                weight_out.reshape(1024, 1024),
                bias_out,
                jnp.transpose(cotangent, (1, 0, 2)),
            )
        )
    )


def solution(mesh):
    return jax.shard_map(
        per_device,
        mesh=mesh,
        in_specs=(
            P("expert", None, "hidden"),
            P("hidden", None),
            P("expert", None, "hidden"),
            P("expert", "hidden"),
            P("expert", "hidden", None),
            P("expert", "hidden"),
            P("expert", None, "hidden"),
        ),
        out_specs=(P("expert", None, "hidden"), P("expert", None, "hidden"), P("expert", None)),
        check_vma=False,
    )
```

```python
import jax
import jax.numpy as jnp
from jax import lax
from jax.experimental import pallas as pl
from jax.experimental.pallas import tpu as pltpu
from jax.sharding import PartitionSpec as P

loss_weight = 0.1
MESH = pl.DeviceIdType.MESH
F32, BF16 = jnp.float32, jnp.bfloat16

IMG, TOK, TP, HALF, QF, SLOTS = 2, 196, 208, 104, 256, 128
NJ, NZ, NZL = 16, 16, 8


def gelu_parts(value):
    factor = 0.7978845608028654
    inner = factor * (value + 0.044715 * value * value * value)
    slope_tanh = jnp.tanh(inner)
    result = 0.5 * value * (1.0 + slope_tanh)
    slope = 0.5 * (1.0 + slope_tanh) + 0.5 * value * (1.0 - slope_tanh * slope_tanh) * factor * (
        1.0 + 3.0 * 0.044715 * value * value
    )
    return result, slope


def dot(a, b, ca, cb):
    return lax.dot_general(a, b, (((ca,), (cb,)), ((), ())), preferred_element_type=F32)


def kernel(
    tok_hbm, sp_hbm, w1_hbm, bi_hbm, w2_hbm, bo_hbm, cot_hbm,
    mixed, tgrad, zloss,
    tok_in, sp, w1, bi, w2, bo, cot_in, insem, tok, cot,
    lp, la, lzs, lzr, lf,
    disp, comb, tcomb, dlow, clow,
    s, r1, fa, r2, x,
    act, slope, part, px_s, px_r, ft, cq, cr, fc, cs, y, fb, v,
    gp, ga, gzs, gzr, gf,
    a1s, a1r, a2s, a2r, a3s, a3r, b1s, b1r, b2s, b2r, fws, fwr,
    pxs, pxr, c1s, c1r, c2s, c2r, d1s, d1r, d2s, d2r, d3s, d3r,
):
    div, rem = lax.div, lax.rem
    e, h = lax.axis_index("expert"), lax.axis_index("hidden")
    j, zl, zh, c = div(e, NZL), rem(e, NZL), div(h, 2), rem(h, 2)
    jy, jx = div(j, 4), rem(j, 4)
    z = zh * NZL + zl
    core_peer = (e, zh * 2 + 1 - c)
    z8_peer = (e, (1 - zh) * 2 + c)

    def z_at(d):
        zz = rem(z + d, NZ)
        return div(zz, NZL), rem(zz, NZL)

    def z_dev(place):
        return (j * NZL + place[1], place[0] * 2 + c)

    def j_at(d):
        return rem(jy + d // 4, 4) * 4 + rem(jx + d % 4, 4)

    def j_dev(jj):
        return (jj * NZL + zl, h)

    def rc(src, dst, ss, rs, dev):
        return pltpu.make_async_remote_copy(
            src_ref=src, dst_ref=dst, send_sem=ss, recv_sem=rs, device_id=dev, device_id_type=MESH
        )

    along_z = (8, 7, 9, 6, 10, 5, 11, 4, 12, 3, 13, 2, 14, 1, 15)
    in_plane = (10, 6, 14, 9, 11, 5, 7, 13, 15, 2, 8, 1, 3, 4, 12)

    def each(steps, body):
        for d in steps:
            body(d)

    barrier = pltpu.get_barrier_semaphore()

    def greet(dev):
        pl.semaphore_signal(barrier, inc=1, device_id=dev, device_id_type=MESH)

    given = (tok_hbm, sp_hbm, cot_hbm, w1_hbm, bi_hbm, w2_hbm, bo_hbm)
    kept = (tok_in, sp, cot_in, w1, bi, w2, bo)
    loads = [pltpu.make_async_copy(a, b, insem.at[k]) for k, (a, b) in enumerate(zip(given, kept))]
    greet(z8_peer)
    loads[0].start()
    loads[1].start()
    each(along_z[1:], lambda d: greet(z_dev(z_at(d))))
    each(in_plane, lambda d: greet(j_dev(j_at(d))))
    greet(core_peer)
    for load in loads[2:]:
        load.start()

    mine, theirs = pl.ds(pl.multiple_of(c * HALF, 8), HALF), pl.ds(pl.multiple_of((1 - c) * HALF, 8), HALF)

    def laid_out(given, kept):
        for i in range(IMG):
            kept[i, TP - 16 : TP, :] = jnp.zeros((16, QF), BF16)
        whole = given[...].astype(F32)
        for i in range(IMG):
            kept[i, 0:TOK, :] = whole[:, i, :].astype(BF16)

    loads[0].wait()
    laid_out(tok_in, tok)
    loads[1].wait()
    for i in range(IMG):
        lp[i] = dot(tok[i], sp[...], 1, 0)
    pl.semaphore_wait(barrier, 1 + (NZ - 1) + (NJ - 1))

    def a1(i):
        return rc(lp.at[i, theirs], la.at[i], a1s.at[i], a1r.at[i], core_peer)

    def a2(i):
        return rc(lzs.at[i], lzr.at[i], a2s.at[i], a2r.at[i], z8_peer)

    def a3(i, rows):
        return rc(lf.at[i, rows], lf.at[i, rows], a3s.at[i], a3r.at[i], core_peer)

    def b1(i, t, src, dst, dev):
        return rc(s.at[i, t, src], r1.at[i, t, dst], b1s.at[i, t], b1r.at[i, t], dev)

    def b2(i, t, place):
        return rc(
            r2.at[i, t, place[1]], x.at[i, t, (zh * 2 + c) * NZL + zl], b2s.at[i, t], b2r.at[i, t], z_dev(place)
        )

    def fwd(i, t, half, core):
        there = x.at[i, t, pl.ds((half * 2 + core) * NZL, NZL)]
        return rc(there, there, fws.at[i, t, half], fwr.at[i, t, half], core_peer)

    def px(i, t):
        return rc(px_s.at[i, t], px_r.at[i, t], pxs.at[i, t], pxr.at[i, t], core_peer)

    def c1(i, t, dst, dev):
        return rc(cq.at[i, t, dst], cr.at[i, t, j], c1s.at[i, t], c1r.at[i, t], dev)

    def c2(i, t, place):
        return rc(cs.at[i, t, place[0] * NZL + place[1]], y.at[i, t, z], c2s.at[i, t], c2r.at[i, t], z_dev(place))

    fifteen = pl.ds(0, 15)

    def b1_all(i, t):
        return rc(s.at[i, t, fifteen], r1.at[i, t, fifteen], b1s.at[i, t], b1r.at[i, t], core_peer)

    def b2_all(i, t):
        return rc(x.at[i, t, fifteen], x.at[i, t, fifteen], b2s.at[i, t], b2r.at[i, t], core_peer)

    def c1_all(i, t):
        return rc(cq.at[i, t, fifteen], cr.at[i, t, fifteen], c1s.at[i, t], c1r.at[i, t], core_peer)

    def c2_all(i, t):
        return rc(cs.at[i, t, fifteen], y.at[i, t, fifteen], c2s.at[i, t], c2r.at[i, t], core_peer)

    def d1(i):
        return rc(gp.at[i, theirs], ga.at[i], d1s.at[i], d1r.at[i], core_peer)

    def d2(i):
        return rc(gzs.at[i], gzr.at[i], d2s.at[i], d2r.at[i], z8_peer)

    def d3(i, rows):
        return rc(gf.at[i, rows], gf.at[i, rows], d3s.at[i], d3r.at[i], core_peer)

    def logits_across(i):
        a1(i).wait_recv()
        lzs[i] = lp[i, mine] + la[i]
        if i == 0:
            a2(i).start()

    def logits_whole(i):
        a2(i).wait_recv()
        lf[i, mine] = lzs[i] + lzr[i]
        a3(i, mine).start()
        if i == 0:
            a2(1).start()

    def send_slots(i, t):
        each(in_plane, lambda d: b1(i, t, j_at(d), j, j_dev(j_at(d))).start())
        r1[i, t, j] = s[i, t, j]

    def dispatches(i):
        a3(i, theirs).wait_recv()
        row = lax.broadcasted_iota(jnp.int32, (TP, SLOTS), 0)
        masked = jnp.where(row < TOK, lf[i], -1e30)
        top = jnp.max(masked, axis=0, keepdims=True)
        up = jnp.exp(masked - top)
        dispatch = up / jnp.sum(up, axis=0, keepdims=True)
        disp[i] = dispatch
        dispatch_low = dispatch.astype(BF16)
        dlow[i] = dispatch_low
        s[i, 0] = dot(dispatch_low, tok[i], 0, 0).reshape(NJ, 8, QF).astype(BF16)
        send_slots(i, 0)

    def combines(i):
        logits = lf[i]
        top = jnp.max(logits, axis=1, keepdims=True)
        up = jnp.exp(logits - top)
        below = jnp.sum(up, axis=1, keepdims=True)
        combine = up / below
        comb[i] = combine
        combine_low = combine.astype(BF16)
        clow[i] = combine_low
        s[i, 1] = dot(combine_low, cot[i], 0, 0).reshape(NJ, 8, QF).astype(BF16)
        send_slots(i, 1)
        total = top + jnp.log(below)
        tcomb[i] = (2.0 * loss_weight) * total * combine
        wide = jnp.broadcast_to(loss_weight * total * total, (TP, SLOTS))
        zloss[i : i + 1, :] = jnp.transpose(wide)[0:1, 0:TOK]

    def to_experts(i, t):
        b1_all(i, t).wait_recv()
        rows = r1[i, t].astype(F32).reshape(SLOTS, QF)
        for lanes in range(2):
            fa[t, lanes] = rows[:, lanes * 128 : (lanes + 1) * 128]
        for low in range(NZL):
            rows = [fa[t, lanes, pl.ds(low, NJ, stride=8), :] for lanes in range(2)]
            r2[i, t, low] = jnp.concatenate(rows, axis=1).astype(BF16)
        each(along_z, lambda k: b2(i, t, z_at(k)).start())
        x[i, t, h * NZL + zl] = r2[i, t, zl]

    def arrive(i, t):
        b2_all(i, t).wait_recv()
        for half in range(2):
            fwd(i, t, half, c).start()

    def quarter(k, core):
        return pl.ds(pl.multiple_of((k * 2 + core) * QF, QF), QF)

    FB = 256

    def by_features(i, t, core, product):
        arrived = [x[i, t, pl.ds((k * 2 + core) * NZL, NZL)].reshape(SLOTS, QF) for k in range(2)]
        for f in range(0, 1024, FB):
            yield f, sum(product(arrived[k], quarter(k, core), f) for k in range(2))

    def project(i, t, product):
        for f, total in by_features(i, t, c, product):
            part[:, f : f + FB] = total
        for half in range(2):
            fwd(i, t, half, 1 - c).wait_recv()
        for f, total in by_features(i, t, 1 - c, product):
            yield f, part[:, f : f + FB] + total

    def expert_out(i):
        def product(rows, features, f):
            return dot(rows, w1[features, f : f + FB], 1, 0)

        for f, total in project(i, 0, product):
            activated, slope_part = gelu_parts(total + bi[:, f : f + FB].astype(F32))
            act[0, :, f : f + FB] = activated.astype(BF16)
            slope[:, f : f + FB] = slope_part
        send_results(i, 0, lambda cols: dot(act[0], w2[:, cols], 1, 0))

    def expert_grad(i):
        def product(rows, features, f):
            return dot(rows, w2[f : f + FB, features], 1, 1)

        for f, total in project(i, 1, product):
            act[1, :, f : f + FB] = (total * slope[:, f : f + FB]).astype(BF16)
        send_results(i, 1, lambda cols: dot(act[1], w1[cols, :], 1, 1))

    def send_results(i, t, product):
        for k in range(2):
            px_s[i, t, k] = product(quarter(k, 1 - c)).astype(BF16)
        px(i, t).start()
        own = [product(quarter(k, c)) for k in range(2)]
        px(i, t).wait_recv()
        for k in range(2):
            total = own[k] + px_r[i, t, k].astype(F32)
            if t == 0:
                total = total + jnp.where(zh == k, 1.0, 0.0) * bo[...].astype(F32)
            for lanes in range(2):
                ft[k, lanes] = total[:, lanes * 128 : (lanes + 1) * 128]
        for dst in range(NJ):
            for k in range(2):
                rows = [ft[k, lanes, pl.ds(dst, 8, stride=NJ), :] for lanes in range(2)]
                cq[i, t, dst, k] = jnp.concatenate(rows, axis=1).astype(BF16)
        each(in_plane, lambda d: c1(i, t, j_at(d), j_dev(j_at(d))).start())
        cr[i, t, j] = cq[i, t, j]

    def turn(i, t):
        c1_all(i, t).wait_recv()
        for k in range(2):
            rows = cr[i, t, :, k].astype(F32).reshape(SLOTS, QF)
            for lanes in range(2):
                fc[k, lanes] = rows[:, lanes * 128 : (lanes + 1) * 128]
        for k in range(2):
            for low in range(NZL):
                rows = [fc[k, lanes, pl.ds(low, NJ, stride=8), :] for lanes in range(2)]
                cs[i, t, k * NZL + low] = jnp.concatenate(rows, axis=1).astype(BF16)
        each(along_z, lambda k: c2(i, t, z_at(k)).start())
        y[i, t, z] = cs[i, t, z]

    def home(i, t):
        c2_all(i, t).wait_recv()
        for low in range(NZL):
            rows = y[i, t, low].astype(F32) + y[i, t, NZL + low].astype(F32)
            for lanes in range(2):
                fb[lanes, pl.ds(low, NJ, stride=8), :] = rows[:, lanes * 128 : (lanes + 1) * 128]
        v[i, t] = jnp.concatenate([fb[lanes] for lanes in range(2)], axis=1).astype(BF16)

    def outputs(i):
        slot_out = v[i, 0]
        mixed[i] = dot(clow[i], slot_out, 1, 0).astype(BF16)[0:TOK, :]
        combine_grad = dot(cot[i], slot_out, 1, 1)
        combine = comb[i]
        gp[i] = combine * (combine_grad - jnp.sum(combine * combine_grad, axis=1, keepdims=True))

    def gradients(i):
        dispatch_grad = dot(tok[i], v[i, 1], 1, 1)
        dispatch = disp[i]
        gp[i] += dispatch * (dispatch_grad - jnp.sum(dispatch * dispatch_grad, axis=0, keepdims=True))
        d1(i).start()

    def gradients_across(i):
        d1(i).wait_recv()
        half = gp[i, mine] + ga[i]
        gzs[i] = half.astype(BF16)
        d2(i).start()
        ga[i] = half + tcomb[i, mine]

    def gradients_whole(i):
        d2(i).wait_recv()
        half = ga[i] + gzr[i].astype(F32)
        gf[i, mine] = half.astype(BF16).astype(F32)
        d3(i, mine).start()

    def finish(i):
        result = dot(dlow[i], v[i, 1], 1, 0)
        d3(i, theirs).wait_recv()
        tgrad[i] = (result + dot(gf[i].astype(BF16), sp[...], 1, 1)).astype(BF16)[0:TOK, :]

    for copy in [a1(i) for i in range(IMG)]:
        copy.start()
    logits_across(0)
    logits_across(1)
    loads[2].wait()
    laid_out(cot_in, cot)
    logits_whole(0)
    dispatches(0)
    combines(0)
    to_experts(0, 0)
    to_experts(0, 1)
    logits_whole(1)
    dispatches(1)
    combines(1)
    to_experts(1, 0)
    to_experts(1, 1)
    for load in loads[3:]:
        load.wait()
    arrive(0, 0)
    expert_out(0)
    arrive(0, 1)
    expert_grad(0)
    turn(0, 0)
    arrive(1, 0)
    expert_out(1)
    turn(0, 1)
    arrive(1, 1)
    expert_grad(1)
    turn(1, 0)
    turn(1, 1)
    home(0, 0)
    outputs(0)
    home(0, 1)
    gradients(0)
    gradients_across(0)
    home(1, 0)
    outputs(1)
    home(1, 1)
    gradients(1)
    gradients_across(1)
    gradients_whole(0)
    finish(0)
    for i in range(IMG):
        for copy in (a1(i), a2(i), a3(i, mine), d1(i), d2(i)):
            copy.wait_send()
        for t in range(2):
            for copy in (b1_all(i, t), b2_all(i, t), fwd(i, t, 0, c), fwd(i, t, 1, c)):
                copy.wait_send()
            for copy in (px(i, t), c1_all(i, t), c2_all(i, t)):
                copy.wait_send()
    gradients_whole(1)
    finish(1)
    d3(0, mine).wait_send()
    d3(1, mine).wait_send()


def deliver(mixed_in, tgrad_in, zloss_in, mixed, tgrad, zloss):
    for given, wanted in ((mixed_in, mixed), (tgrad_in, tgrad)):
        both = [given[i].astype(F32) for i in range(IMG)]
        wanted[...] = jnp.stack(both, axis=1).astype(BF16)
    zloss[...] = zloss_in[...]


def per_device(tokens, slot_params, weight_in, bias_in, weight_out, bias_out, cotangent):
    vmem = pl.BlockSpec(memory_space=pltpu.VMEM)
    hbm = pl.BlockSpec(memory_space=pltpu.HBM)
    dma = pltpu.SemaphoreType.DMA
    scratch = [
        ((TOK, IMG, QF), BF16),
        ((QF, SLOTS), BF16),
        ((1024, 1024), BF16),
        ((1, 1024), BF16),
        ((1024, 1024), BF16),
        ((1, QF), BF16),
        ((TOK, IMG, QF), BF16),
        dma((7,)),
        ((IMG, TP, QF), BF16),
        ((IMG, TP, QF), BF16),
        ((IMG, TP, SLOTS), F32),
        ((IMG, HALF, SLOTS), F32),
        ((IMG, HALF, SLOTS), F32),
        ((IMG, HALF, SLOTS), F32),
        ((IMG, TP, SLOTS), F32),
        ((IMG, TP, SLOTS), F32),
        ((IMG, TP, SLOTS), F32),
        ((IMG, TP, SLOTS), F32),
        ((IMG, TP, SLOTS), BF16),
        ((IMG, TP, SLOTS), BF16),
        ((IMG, 2, NJ, 8, QF), BF16),
        ((IMG, 2, NJ, 8, QF), BF16),
        ((2, 2, SLOTS, 128), F32),
        ((IMG, 2, NZL, NJ, QF), BF16),
        ((IMG, 2, 4 * NZL, NJ, QF), BF16),
        ((2, SLOTS, 1024), BF16),
        ((SLOTS, 1024), F32),
        ((SLOTS, 1024), F32),
        ((IMG, 2, 2, SLOTS, QF), BF16),
        ((IMG, 2, 2, SLOTS, QF), BF16),
        ((2, 2, SLOTS, 128), F32),
        ((IMG, 2, NJ, 2, 8, QF), BF16),
        ((IMG, 2, NJ, 2, 8, QF), BF16),
        ((2, 2, SLOTS, 128), F32),
        ((IMG, 2, NZ, NJ, QF), BF16),
        ((IMG, 2, NZ, NJ, QF), BF16),
        ((2, SLOTS, 128), F32),
        ((IMG, 2, SLOTS, QF), BF16),
        ((IMG, TP, SLOTS), F32),
        ((IMG, HALF, SLOTS), F32),
        ((IMG, HALF, SLOTS), BF16),
        ((IMG, HALF, SLOTS), BF16),
        ((IMG, TP, SLOTS), F32),
    ]
    scratch = [pltpu.VMEM(*a) if isinstance(a, tuple) else a for a in scratch]
    scratch += [dma((IMG,))] * 6 + [dma((IMG, 2))] * 4 + [dma((IMG, 2, 2))] * 2 + [dma((IMG, 2))] * 6 + [dma((IMG,))] * 6
    done = pl.pallas_call(
        kernel,
        out_shape=(
            jax.ShapeDtypeStruct((IMG, TOK, QF), BF16),
            jax.ShapeDtypeStruct((IMG, TOK, QF), BF16),
            jax.ShapeDtypeStruct((IMG, TOK), F32),
        ),
        in_specs=[hbm] * 7,
        out_specs=(vmem, vmem, vmem),
        scratch_shapes=scratch,
        compiler_params=pltpu.CompilerParams(
            collective_id=1, has_side_effects=True, vmem_limit_bytes=20 * 2**20
        ),
        name="layer",
    )(
        *(
            pltpu.with_memory_space_constraint(given, pltpu.HBM)
            for given in (
                jnp.transpose(tokens, (1, 0, 2)),
                slot_params,
                weight_in.reshape(1024, 1024),
                bias_in,
                weight_out.reshape(1024, 1024),
                bias_out,
                jnp.transpose(cotangent, (1, 0, 2)),
            )
        )
    )
    mixed, token_grad, zloss = pl.pallas_call(
        deliver,
        out_shape=(
            jax.ShapeDtypeStruct((TOK, IMG, QF), BF16),
            jax.ShapeDtypeStruct((TOK, IMG, QF), BF16),
            jax.ShapeDtypeStruct((IMG, TOK), F32),
        ),
        in_specs=[vmem] * 3,
        out_specs=(vmem, vmem, vmem),
        compiler_params=pltpu.CompilerParams(vmem_limit_bytes=20 * 2**20),
        name="deliver",
    )(*done)
    return jnp.transpose(mixed, (1, 0, 2)), jnp.transpose(token_grad, (1, 0, 2)), zloss


def solution(mesh):
    return jax.shard_map(
        per_device,
        mesh=mesh,
        in_specs=(
            P("expert", None, "hidden"),
            P("hidden", None),
            P("expert", None, "hidden"),
            P("expert", "hidden"),
            P("expert", "hidden", None),
            P("expert", "hidden"),
            P("expert", None, "hidden"),
        ),
        out_specs=(P("expert", None, "hidden"), P("expert", None, "hidden"), P("expert", None)),
        check_vma=False,
    )
```

```python
import jax
import jax.numpy as jnp
from jax import lax
from jax.experimental import pallas as pl
from jax.experimental.pallas import tpu as pltpu
from jax.sharding import PartitionSpec as P

loss_weight = 0.1
MESH = pl.DeviceIdType.MESH
F32, BF16 = jnp.float32, jnp.bfloat16

IMG, TOK, TP, HALF, QF, SLOTS = 2, 196, 208, 104, 256, 128
NJ, NZ, NZL = 16, 16, 8


def gelu_parts(value):
    factor = 0.7978845608028654
    inner = factor * (value + 0.044715 * value * value * value)
    slope_tanh = jnp.tanh(inner)
    result = 0.5 * value * (1.0 + slope_tanh)
    slope = 0.5 * (1.0 + slope_tanh) + 0.5 * value * (1.0 - slope_tanh * slope_tanh) * factor * (
        1.0 + 3.0 * 0.044715 * value * value
    )
    return result, slope


def dot(a, b, ca, cb):
    return lax.dot_general(a, b, (((ca,), (cb,)), ((), ())), preferred_element_type=F32)


def kernel(
    tok_hbm, sp_hbm, w1_hbm, bi_hbm, w2_hbm, bo_hbm, cot_hbm,
    mixed, tgrad, zloss,
    tok_in, sp, w1, bi, w2, bo, cot_in, insem, tok, cot,
    lp, la, lzs, lzr, lf,
    disp, comb, tcomb, dlow, clow,
    s, r1, fa, r2, x, wz, fw, xs, x0,
    act, slope, part, px_s, px_r, ft, cq, cr, fc, cs, y, fb, v,
    gp, ga, gzs, gzr, gf,
    a1s, a1r, a2s, a2r, a3s, a3r, b1s, b1r, b2s, b2r, fws, fwr,
    pxs, pxr, c1s, c1r, c2s, c2r, d1s, d1r, d2s, d2r, d3s, d3r,
):
    div, rem = lax.div, lax.rem
    e, h = lax.axis_index("expert"), lax.axis_index("hidden")
    j, zl, zh, c = div(e, NZL), rem(e, NZL), div(h, 2), rem(h, 2)
    jy, jx = div(j, 4), rem(j, 4)
    z = zh * NZL + zl
    core_peer = (e, zh * 2 + 1 - c)
    z8_peer = (e, (1 - zh) * 2 + c)

    def z_at(d):
        zz = rem(z + d, NZ)
        return div(zz, NZL), rem(zz, NZL)

    def z_dev(place):
        return (j * NZL + place[1], place[0] * 2 + c)

    def j_at(d):
        return rem(jy + d // 4, 4) * 4 + rem(jx + d % 4, 4)

    def j_dev(jj):
        return (jj * NZL + zl, h)

    def rc(src, dst, ss, rs, dev):
        return pltpu.make_async_remote_copy(
            src_ref=src, dst_ref=dst, send_sem=ss, recv_sem=rs, device_id=dev, device_id_type=MESH
        )

    along_z = (8, 7, 9, 6, 10, 5, 11, 4, 12, 3, 13, 2, 14, 1, 15)
    in_plane = (10, 6, 14, 9, 11, 5, 7, 13, 15, 2, 8, 1, 3, 4, 12)

    def each(steps, body):
        for d in steps:
            body(d)

    barrier = pltpu.get_barrier_semaphore()

    def greet(dev):
        pl.semaphore_signal(barrier, inc=1, device_id=dev, device_id_type=MESH)

    given = (tok_hbm, sp_hbm, cot_hbm, w1_hbm, bi_hbm, w2_hbm, bo_hbm)
    kept = (tok_in, sp, cot_in, w1, bi, w2, bo)
    loads = [pltpu.make_async_copy(a, b, insem.at[k]) for k, (a, b) in enumerate(zip(given, kept))]
    greet(z8_peer)
    loads[0].start()
    loads[1].start()
    each(along_z[1:], lambda d: greet(z_dev(z_at(d))))
    each(in_plane, lambda d: greet(j_dev(j_at(d))))
    greet(core_peer)
    for load in loads[2:]:
        load.start()

    mine, theirs = pl.ds(pl.multiple_of(c * HALF, 8), HALF), pl.ds(pl.multiple_of((1 - c) * HALF, 8), HALF)

    def laid_out(given, kept):
        for i in range(IMG):
            kept[i, TP - 16 : TP, :] = jnp.zeros((16, QF), BF16)
        whole = given[...].astype(F32)
        for i in range(IMG):
            kept[i, 0:TOK, :] = whole[:, i, :].astype(BF16)

    loads[0].wait()
    laid_out(tok_in, tok)
    loads[1].wait()
    for i in range(IMG):
        lp[i] = dot(tok[i], sp[...], 1, 0)
    pl.semaphore_wait(barrier, 1 + (NZ - 1) + (NJ - 1))

    def a1(i):
        return rc(lp.at[i, theirs], la.at[i], a1s.at[i], a1r.at[i], core_peer)

    def a2(i):
        return rc(lzs.at[i], lzr.at[i], a2s.at[i], a2r.at[i], z8_peer)

    def a3(i, rows):
        return rc(lf.at[i, rows], lf.at[i, rows], a3s.at[i], a3r.at[i], core_peer)

    def b1(i, t, dst, dev):
        out, into = (s.at[i, t, dst], r1.at[i, t, j]) if i else (xs.at[t, dst], x0.at[t, 0, j])
        return rc(out, into, b1s.at[i, t], b1r.at[i, t], dev)

    def b2(i, t, place):
        into = x.at[t, (zh * 2 + c) * NZL + zl] if i else wz.at[t, z]
        return rc(r2.at[i, t, place[1]], into, b2s.at[i, t], b2r.at[i, t], z_dev(place))

    def fwd(i, t, half, core):
        if i == 0:
            return rc(x0.at[t, 0, :, half], x0.at[t, 1, :, half], fws.at[i, t, half], fwr.at[i, t, half], core_peer)
        there = x.at[t, pl.ds((half * 2 + core) * NZL, NZL)]
        return rc(there, there, fws.at[i, t, half], fwr.at[i, t, half], core_peer)

    def px(i, t):
        return rc(px_s.at[i, t], px_r.at[i, t], pxs.at[i, t], pxr.at[i, t], core_peer)

    def c1(i, t, dst, dev):
        return rc(cq.at[i, t, dst], cr.at[i, t, j], c1s.at[i, t], c1r.at[i, t], dev)

    def c2(i, t, place):
        return rc(cs.at[i, t, place[0] * NZL + place[1]], y.at[i, t, z], c2s.at[i, t], c2r.at[i, t], z_dev(place))

    fifteen = pl.ds(0, 15)

    def b1_all(i, t):
        out, into = (s.at[i, t], r1.at[i, t]) if i else (xs.at[t], x0.at[t, 0])
        return rc(out.at[fifteen], into.at[fifteen], b1s.at[i, t], b1r.at[i, t], core_peer)

    def b2_all(i, t):
        into = x.at[t, fifteen] if i else wz.at[t, fifteen]
        return rc(into, into, b2s.at[i, t], b2r.at[i, t], core_peer)

    def c1_all(i, t):
        return rc(cq.at[i, t, fifteen], cr.at[i, t, fifteen], c1s.at[i, t], c1r.at[i, t], core_peer)

    def c2_all(i, t):
        return rc(cs.at[i, t, fifteen], y.at[i, t, fifteen], c2s.at[i, t], c2r.at[i, t], core_peer)

    def d1(i):
        return rc(gp.at[i, theirs], ga.at[i], d1s.at[i], d1r.at[i], core_peer)

    def d2(i):
        return rc(gzs.at[i], gzr.at[i], d2s.at[i], d2r.at[i], z8_peer)

    def d3(i, rows):
        return rc(gf.at[i, rows], gf.at[i, rows], d3s.at[i], d3r.at[i], core_peer)

    def logits_across(i):
        a1(i).wait_recv()
        lzs[i] = lp[i, mine] + la[i]
        a2(i).start()

    def logits_whole(i):
        a2(i).wait_recv()
        lf[i, mine] = lzs[i] + lzr[i]
        a3(i, mine).start()

    def send_along_z(i, t, rows):
        for lanes in range(2):
            fa[t, lanes] = rows[:, lanes * 128 : (lanes + 1) * 128]
        for low in range(NZL):
            rows = [fa[t, lanes, pl.ds(low, NJ, stride=8), :] for lanes in range(2)]
            r2[i, t, low] = jnp.concatenate(rows, axis=1).astype(BF16)
        each(along_z, lambda k: b2(i, t, z_at(k)).start())
        if i:
            x[t, h * NZL + zl] = r2[i, t, zl]
        else:
            wz[t, z] = r2[i, t, zl]

    def send_slots(i, t, rows):
        if i == 0:
            send_along_z(i, t, rows)
            return
        s[i, t] = rows.reshape(NJ, 8, QF).astype(BF16)
        each(in_plane, lambda d: b1(i, t, j_at(d), j_dev(j_at(d))).start())
        r1[i, t, j] = s[i, t, j]

    def dispatches(i):
        a3(i, theirs).wait_recv()
        row = lax.broadcasted_iota(jnp.int32, (TP, SLOTS), 0)
        masked = jnp.where(row < TOK, lf[i], -1e30)
        top = jnp.max(masked, axis=0, keepdims=True)
        up = jnp.exp(masked - top)
        dispatch = up / jnp.sum(up, axis=0, keepdims=True)
        disp[i] = dispatch
        dispatch_low = dispatch.astype(BF16)
        dlow[i] = dispatch_low
        send_slots(i, 0, dot(dispatch_low, tok[i], 0, 0))

    def combines(i):
        logits = lf[i]
        top = jnp.max(logits, axis=1, keepdims=True)
        up = jnp.exp(logits - top)
        below = jnp.sum(up, axis=1, keepdims=True)
        combine = up / below
        comb[i] = combine
        combine_low = combine.astype(BF16)
        clow[i] = combine_low
        send_slots(i, 1, dot(combine_low, cot[i], 0, 0))
        total = top + jnp.log(below)
        tcomb[i] = (2.0 * loss_weight) * total * combine
        wide = jnp.broadcast_to(loss_weight * total * total, (TP, SLOTS))
        zloss[i : i + 1, :] = jnp.transpose(wide)[0:1, 0:TOK]

    def to_experts(i, t):
        b1_all(i, t).wait_recv()
        send_along_z(i, t, r1[i, t].astype(F32).reshape(SLOTS, QF))

    def cross(t):
        b2_all(0, t).wait_recv()
        for k in range(2):
            rows = wz[t, k * NZL : (k + 1) * NZL].astype(F32).reshape(SLOTS, QF)
            for lanes in range(2):
                fw[k, lanes] = rows[:, lanes * 128 : (lanes + 1) * 128]
        for dst in range(NJ):
            for k in range(2):
                rows = [fw[k, lanes, pl.ds(dst, 8, stride=NJ), :] for lanes in range(2)]
                xs[t, dst, k] = jnp.concatenate(rows, axis=1).astype(BF16)
        each(in_plane, lambda d: b1(0, t, j_at(d), j_dev(j_at(d))).start())
        x0[t, 0, j] = xs[t, j]

    def arrive(i, t):
        (b2_all if i else b1_all)(i, t).wait_recv()
        for half in range(2):
            fwd(i, t, half, c).start()

    def quarter(k, core):
        return pl.ds(pl.multiple_of((k * 2 + core) * QF, QF), QF)

    FB = 256

    def by_features(i, t, side, product):
        core = (1 - c) if side else c
        if i == 0:
            arrived = [x0[t, side, :, k].astype(F32).reshape(SLOTS, QF).astype(BF16) for k in range(2)]
        else:
            arrived = [x[t, pl.ds((k * 2 + core) * NZL, NZL)].reshape(SLOTS, QF) for k in range(2)]
        for f in range(0, 1024, FB):
            yield f, sum(product(arrived[k], quarter(k, core), f) for k in range(2))

    def project(i, t, product):
        for f, total in by_features(i, t, 0, product):
            part[:, f : f + FB] = total
        for half in range(2):
            fwd(i, t, half, 1 - c).wait_recv()
        for f, total in by_features(i, t, 1, product):
            yield f, part[:, f : f + FB] + total

    def expert_out(i):
        def product(rows, features, f):
            return dot(rows, w1[features, f : f + FB], 1, 0)

        for f, total in project(i, 0, product):
            activated, slope_part = gelu_parts(total + bi[:, f : f + FB].astype(F32))
            act[0, :, f : f + FB] = activated.astype(BF16)
            slope[:, f : f + FB] = slope_part
        send_results(i, 0, lambda cols: dot(act[0], w2[:, cols], 1, 0))

    def expert_grad(i):
        def product(rows, features, f):
            return dot(rows, w2[f : f + FB, features], 1, 1)

        for f, total in project(i, 1, product):
            act[1, :, f : f + FB] = (total * slope[:, f : f + FB]).astype(BF16)
        send_results(i, 1, lambda cols: dot(act[1], w1[cols, :], 1, 1))

    def send_results(i, t, product):
        for k in range(2):
            px_s[i, t, k] = product(quarter(k, 1 - c)).astype(BF16)
        px(i, t).start()
        own = [product(quarter(k, c)) for k in range(2)]
        px(i, t).wait_recv()
        for k in range(2):
            total = own[k] + px_r[i, t, k].astype(F32)
            if t == 0:
                total = total + jnp.where(zh == k, 1.0, 0.0) * bo[...].astype(F32)
            if i == 0:
                cq[i, t, :, k] = total.reshape(NJ, 8, QF).astype(BF16)
                continue
            for lanes in range(2):
                ft[k, lanes] = total[:, lanes * 128 : (lanes + 1) * 128]
        for dst in range(NJ if i else 0):
            for k in range(2):
                rows = [ft[k, lanes, pl.ds(dst, 8, stride=NJ), :] for lanes in range(2)]
                cq[i, t, dst, k] = jnp.concatenate(rows, axis=1).astype(BF16)
        each(in_plane, lambda d: c1(i, t, j_at(d), j_dev(j_at(d))).start())
        cr[i, t, j] = cq[i, t, j]

    def turn(i, t):
        c1_all(i, t).wait_recv()
        for k in range(2):
            rows = cr[i, t, :, k].astype(F32).reshape(SLOTS, QF)
            for lanes in range(2):
                fc[k, lanes] = rows[:, lanes * 128 : (lanes + 1) * 128]
        for k in range(2):
            for low in range(NZL):
                rows = [fc[k, lanes, pl.ds(low, NJ, stride=8), :] for lanes in range(2)]
                cs[i, t, k * NZL + low] = jnp.concatenate(rows, axis=1).astype(BF16)
        each(along_z, lambda k: c2(i, t, z_at(k)).start())
        y[i, t, z] = cs[i, t, z]

    def home(i, t):
        c2_all(i, t).wait_recv()
        for low in range(NZL):
            rows = y[i, t, low].astype(F32) + y[i, t, NZL + low].astype(F32)
            for lanes in range(2):
                fb[lanes, pl.ds(low, NJ, stride=8), :] = rows[:, lanes * 128 : (lanes + 1) * 128]
        v[i, t] = jnp.concatenate([fb[lanes] for lanes in range(2)], axis=1).astype(BF16)

    def outputs(i):
        slot_out = v[i, 0]
        mixed[i] = dot(clow[i], slot_out, 1, 0).astype(BF16)[0:TOK, :]
        combine_grad = dot(cot[i], slot_out, 1, 1)
        combine = comb[i]
        gp[i] = combine * (combine_grad - jnp.sum(combine * combine_grad, axis=1, keepdims=True))

    def gradients(i):
        dispatch_grad = dot(tok[i], v[i, 1], 1, 1)
        dispatch = disp[i]
        gp[i] += dispatch * (dispatch_grad - jnp.sum(dispatch * dispatch_grad, axis=0, keepdims=True))
        d1(i).start()

    def gradients_across(i):
        d1(i).wait_recv()
        half = gp[i, mine] + ga[i]
        gzs[i] = half.astype(BF16)
        d2(i).start()
        ga[i] = half + tcomb[i, mine]

    def gradients_whole(i):
        d2(i).wait_recv()
        half = ga[i] + gzr[i].astype(F32)
        gf[i, mine] = half.astype(BF16).astype(F32)
        d3(i, mine).start()

    def finish(i):
        result = dot(dlow[i], v[i, 1], 1, 0)
        d3(i, theirs).wait_recv()
        tgrad[i] = (result + dot(gf[i].astype(BF16), sp[...], 1, 1)).astype(BF16)[0:TOK, :]

    for copy in [a1(i) for i in range(IMG)]:
        copy.start()
    logits_across(0)
    logits_across(1)
    loads[2].wait()
    laid_out(cot_in, cot)
    logits_whole(0)
    dispatches(0)
    combines(0)
    logits_whole(1)
    dispatches(1)
    combines(1)
    cross(0)
    to_experts(1, 0)
    to_experts(1, 1)
    cross(1)
    for load in loads[3:]:
        load.wait()
    arrive(0, 0)
    expert_out(0)
    arrive(0, 1)
    expert_grad(0)
    turn(0, 0)
    arrive(1, 0)
    expert_out(1)
    turn(0, 1)
    arrive(1, 1)
    expert_grad(1)
    turn(1, 0)
    turn(1, 1)
    home(0, 0)
    outputs(0)
    home(0, 1)
    gradients(0)
    gradients_across(0)
    home(1, 0)
    outputs(1)
    home(1, 1)
    gradients(1)
    gradients_across(1)
    gradients_whole(0)
    finish(0)
    for i in range(IMG):
        for copy in (a1(i), a2(i), a3(i, mine), d1(i), d2(i)):
            copy.wait_send()
        for t in range(2):
            for copy in (b1_all(i, t), b2_all(i, t), fwd(i, t, 0, c), fwd(i, t, 1, c)):
                copy.wait_send()
            for copy in (px(i, t), c1_all(i, t), c2_all(i, t)):
                copy.wait_send()
    gradients_whole(1)
    finish(1)
    d3(0, mine).wait_send()
    d3(1, mine).wait_send()


def deliver(mixed_in, tgrad_in, zloss_in, mixed, tgrad, zloss):
    for given, wanted in ((mixed_in, mixed), (tgrad_in, tgrad)):
        both = [given[i].astype(F32) for i in range(IMG)]
        wanted[...] = jnp.stack(both, axis=1).astype(BF16)
    zloss[...] = zloss_in[...]


def per_device(tokens, slot_params, weight_in, bias_in, weight_out, bias_out, cotangent):
    vmem = pl.BlockSpec(memory_space=pltpu.VMEM)
    hbm = pl.BlockSpec(memory_space=pltpu.HBM)
    dma = pltpu.SemaphoreType.DMA
    scratch = [
        ((TOK, IMG, QF), BF16),
        ((QF, SLOTS), BF16),
        ((1024, 1024), BF16),
        ((1, 1024), BF16),
        ((1024, 1024), BF16),
        ((1, QF), BF16),
        ((TOK, IMG, QF), BF16),
        dma((7,)),
        ((IMG, TP, QF), BF16),
        ((IMG, TP, QF), BF16),
        ((IMG, TP, SLOTS), F32),
        ((IMG, HALF, SLOTS), F32),
        ((IMG, HALF, SLOTS), F32),
        ((IMG, HALF, SLOTS), F32),
        ((IMG, TP, SLOTS), F32),
        ((IMG, TP, SLOTS), F32),
        ((IMG, TP, SLOTS), F32),
        ((IMG, TP, SLOTS), F32),
        ((IMG, TP, SLOTS), BF16),
        ((IMG, TP, SLOTS), BF16),
        ((IMG, 2, NJ, 8, QF), BF16),
        ((IMG, 2, NJ, 8, QF), BF16),
        ((2, 2, SLOTS, 128), F32),
        ((IMG, 2, NZL, NJ, QF), BF16),
        ((2, 4 * NZL, NJ, QF), BF16),
        ((2, NZ, NJ, QF), BF16),
        ((2, 2, SLOTS, 128), F32),
        ((2, NJ, 2, 8, QF), BF16),
        ((2, 2, NJ, 2, 8, QF), BF16),
        ((2, SLOTS, 1024), BF16),
        ((SLOTS, 1024), F32),
        ((SLOTS, 1024), F32),
        ((IMG, 2, 2, SLOTS, QF), BF16),
        ((IMG, 2, 2, SLOTS, QF), BF16),
        ((2, 2, SLOTS, 128), F32),
        ((IMG, 2, NJ, 2, 8, QF), BF16),
        ((IMG, 2, NJ, 2, 8, QF), BF16),
        ((2, 2, SLOTS, 128), F32),
        ((IMG, 2, NZ, NJ, QF), BF16),
        ((IMG, 2, NZ, NJ, QF), BF16),
        ((2, SLOTS, 128), F32),
        ((IMG, 2, SLOTS, QF), BF16),
        ((IMG, TP, SLOTS), F32),
        ((IMG, HALF, SLOTS), F32),
        ((IMG, HALF, SLOTS), BF16),
        ((IMG, HALF, SLOTS), BF16),
        ((IMG, TP, SLOTS), F32),
    ]
    scratch = [pltpu.VMEM(*a) if isinstance(a, tuple) else a for a in scratch]
    scratch += [dma((IMG,))] * 6 + [dma((IMG, 2))] * 4 + [dma((IMG, 2, 2))] * 2 + [dma((IMG, 2))] * 6 + [dma((IMG,))] * 6
    done = pl.pallas_call(
        kernel,
        out_shape=(
            jax.ShapeDtypeStruct((IMG, TOK, QF), BF16),
            jax.ShapeDtypeStruct((IMG, TOK, QF), BF16),
            jax.ShapeDtypeStruct((IMG, TOK), F32),
        ),
        in_specs=[hbm] * 7,
        out_specs=(vmem, vmem, vmem),
        scratch_shapes=scratch,
        compiler_params=pltpu.CompilerParams(
            collective_id=1, has_side_effects=True, vmem_limit_bytes=20 * 2**20
        ),
        name="layer",
    )(
        *(
            pltpu.with_memory_space_constraint(given, pltpu.HBM)
            for given in (
                jnp.transpose(tokens, (1, 0, 2)),
                slot_params,
                weight_in.reshape(1024, 1024),
                bias_in,
                weight_out.reshape(1024, 1024),
                bias_out,
                jnp.transpose(cotangent, (1, 0, 2)),
            )
        )
    )
    mixed, token_grad, zloss = pl.pallas_call(
        deliver,
        out_shape=(
            jax.ShapeDtypeStruct((TOK, IMG, QF), BF16),
            jax.ShapeDtypeStruct((TOK, IMG, QF), BF16),
            jax.ShapeDtypeStruct((IMG, TOK), F32),
        ),
        in_specs=[vmem] * 3,
        out_specs=(vmem, vmem, vmem),
        compiler_params=pltpu.CompilerParams(vmem_limit_bytes=20 * 2**20),
        name="deliver",
    )(*done)
    return jnp.transpose(mixed, (1, 0, 2)), jnp.transpose(token_grad, (1, 0, 2)), zloss


def solution(mesh):
    return jax.shard_map(
        per_device,
        mesh=mesh,
        in_specs=(
            P("expert", None, "hidden"),
            P("hidden", None),
            P("expert", None, "hidden"),
            P("expert", "hidden"),
            P("expert", "hidden", None),
            P("expert", "hidden"),
            P("expert", None, "hidden"),
        ),
        out_specs=(P("expert", None, "hidden"), P("expert", None, "hidden"), P("expert", None)),
        check_vma=False,
    )
```
